128 devices in a mesh: state: 16 (over y, x_lo, core), plane: 8 (over z, x_hi).
Axes of the slice: x: 4 (x_hi: 2, x_lo: 2; x = x_hi * 2 + x_lo), y: 4, z: 4, core: 2. Of those that a mesh axis runs over, the one named last changes fastest.
Arguments:
- coeffs: float32 [2, 16, 128, 3072], P(None, 'state', None, 'plane'), may hold values from -6 to 6
- mask: int32 [128, 3072], P(None, 'plane'), may hold values 0 or 1
- stick_cols: int32 [3072], replicated, may hold values from 0 to 8191, as said below
- core: float32 [128, 64, 128], P('plane'), may hold values from 0.05 to 0.5
Outputs:
- forces: float32 [2, 16, 128, 3072], P(None, 'state', None, 'plane')
The draws below stay inside these ranges and needn't reach their ends.
Inputs may be any that keep to these rules, and one draw needn't show every extreme that they name: `stick_cols`: distinct values; 0 and 8191 are always among them.
All inputs are finite; a program needn't handle non-finite values. No bound on the sum of `mask` on one device may be relied on, other than what follows from the above.
Results may differ from the reference program's by a relative error of at most 0.0003.
Values sent between devices are 32-bit elements; how exact they have to be, the bound alone decides.
A program may use at most 128 MiB of HBM per device.

```python
import math
import jax
import jax.numpy as jnp
from jax import lax

NZ = 128
NX = 64
NY = 128
NSTICK = 3072
STATES = 16


def draw_stick_cols(key, part):
    first, second = jax.random.split(jax.random.fold_in(key, 11))
    middle = 1 + jax.random.permutation(first, NX * NY - 2)[:NSTICK - 2]
    ends = jnp.array([0, NX * NY - 1], dtype=jnp.int32)
    columns = jnp.concatenate([ends, middle.astype(jnp.int32)])
    return jax.random.permutation(second, columns).astype(jnp.int32)


def draw_core(key, part):
    second = jax.random.fold_in(jax.random.fold_in(key, 23), 1)
    logs = jax.random.uniform(second, (NZ, NX, NY), jnp.float32, math.log(0.05), math.log(0.5))
    values = jnp.exp(logs)
    return values.astype(jnp.float32)


def with_ends(values, key, least, high):
    place = [jax.random.randint(jax.random.fold_in(key, axis), (), 0, length) for axis, length in enumerate(values.shape)]
    longest = values.shape.index(max(values.shape))
    neighbour = place[:longest] + [(place[longest] + 1) % values.shape[longest]] + place[longest + 1:]
    return values.at[tuple(place)].set(least).at[tuple(neighbour)].set(high)


def shard_levels(own_key, dims, pieces, low, high):
    loudness, own = 1.0, jax.random.fold_in(own_key, 6)
    for axis_at, parts in pieces:
        steps = jnp.exp(jax.random.uniform(jax.random.fold_in(own, axis_at), (parts,), jnp.float32, low / len(pieces), high / len(pieces)))
        loudness = loudness * jnp.repeat(steps, dims[axis_at] // parts).reshape([-1 if axis == axis_at else 1 for axis in range(len(dims))])
    return loudness


def bell_draw(stream_key, dims, width, reach, cuts=(), held_as=jnp.bfloat16):
    factor_of = shard_levels(stream_key, dims, cuts, -0.22, 0.18) if cuts else 1.0
    values = jax.random.normal(stream_key, dims, jnp.float32) * width * factor_of
    return jnp.minimum(jnp.maximum(values, -reach), reach).astype(held_as)


def setup_inputs(seed: int = 0) -> dict:
    arg_keys = jax.random.split(jax.random.key(seed), 5)
    return {
        "coeffs": bell_draw(arg_keys[0], (2, STATES, NZ, NSTICK), 1.0, 6.0, ((1, 16), (3, 8)), jnp.float32),
        "mask": with_ends((jax.random.randint(arg_keys[1], (NZ, NSTICK), 0, 4) < 3).astype(jnp.int32), jax.random.fold_in(arg_keys[1], 1), 0, 1),
        "stick_cols": draw_stick_cols(jax.random.fold_in(arg_keys[4], 71), 0),
        "core": draw_core(jax.random.fold_in(arg_keys[4], 71), 0),
    }


spacing = 0.5
pbe_kappa = 0.804
pbe_mu = 0.2195

def xc_energy(density, grad_sq):
    exch_const = 0.75 * (3.0 / math.pi) ** (1.0 / 3.0)
    scaled = grad_sq / (4.0 * (3.0 * math.pi ** 2) ** (2.0 / 3.0) * density ** (8.0 / 3.0))
    enhance = 1.0 + pbe_kappa - pbe_kappa / (1.0 + pbe_mu * scaled / pbe_kappa)
    exchange = -exch_const * density ** (4.0 / 3.0) * enhance
    radius = (3.0 / (4.0 * math.pi * density)) ** (1.0 / 3.0)
    correlation = -0.44 * density / (7.8 + radius)
    return exchange + correlation

def xc_parts(density, grads):
    grad_sq = grads[0] * grads[0] + grads[1] * grads[1] + grads[2] * grads[2]
    unused, pullback = jax.vjp(xc_energy, density, grad_sq)
    v_local, de_dg = pullback(jnp.ones_like(density))
    return (v_local, [2.0 * de_dg * grad for grad in grads])

def signed_freq(count):
    index = jnp.arange(count, dtype=jnp.int32)
    signed = jnp.where(index >= count // 2, index - count, index)
    deriv = jnp.where(index == count // 2, 0, signed)
    return (signed.astype(jnp.float32), deriv.astype(jnp.float32))

def reference(coeffs, mask, stick_cols, core):
    cells = NX * NY * NZ
    norm = 1.0 / math.sqrt(4.0 * NSTICK * NZ)
    mask_f = mask.astype(jnp.float32)

    def orbital(state):
        real_part = coeffs[0, state] * mask_f
        imag_part = coeffs[1, state] * mask_f
        empty = jnp.zeros((NZ, NX * NY), jnp.float32)
        grid_real = empty.at[:, stick_cols].set(real_part).reshape(NZ, NX, NY)
        grid_imag = empty.at[:, stick_cols].set(imag_part).reshape(NZ, NX, NY)
        return jnp.fft.ifftn(lax.complex(grid_real, grid_imag)) * (cells * norm)

    def accumulate(total, state):
        wave = orbital(state)
        return (total + jnp.real(wave) ** 2 + jnp.imag(wave) ** 2, 0)
    total, unused = lax.scan(accumulate, jnp.zeros((NZ, NX, NY), jnp.float32), jnp.arange(STATES, dtype=jnp.int32))
    density = core + total / STATES
    sz, dz = signed_freq(NZ)
    sx, dx = signed_freq(NX)
    sy, dy = signed_freq(NY)
    fz = 2.0 * math.pi / (NZ * spacing)
    fx = 2.0 * math.pi / (NX * spacing)
    fy = 2.0 * math.pi / (NY * spacing)
    deriv_z = (dz * fz)[:, None, None]
    deriv_x = (dx * fx)[None, :, None]
    deriv_y = (dy * fy)[None, None, :]
    g_sq = (sz * fz)[:, None, None] ** 2 + (sx * fx)[None, :, None] ** 2 + (sy * fy)[None, None, :] ** 2
    hart = jnp.where(g_sq > 0, 4.0 * math.pi / jnp.where(g_sq > 0, g_sq, 1.0), 0.0)
    rho_hat = jnp.fft.fftn(density)
    derivs = [deriv_z, deriv_x, deriv_y]
    grads = [jnp.real(jnp.fft.ifftn(1j * deriv * rho_hat)) for deriv in derivs]
    v_local, fluxes = xc_parts(density, grads)
    combined = hart * rho_hat
    for deriv, flux in zip(derivs, fluxes):
        combined = combined - 1j * deriv * jnp.fft.fftn(flux)
    potential = v_local + jnp.real(jnp.fft.ifftn(combined))

    def force(state):
        wave = orbital(state)
        spectrum = jnp.fft.fftn(potential * wave).reshape(NZ, NX * NY)[:, stick_cols]
        factor = -mask_f / (cells * norm)
        return jnp.stack([jnp.real(spectrum) * factor, jnp.imag(spectrum) * factor])
    result = lax.map(force, jnp.arange(STATES, dtype=jnp.int32))
    return jnp.transpose(result, (1, 0, 2, 3)).astype(jnp.float32)
```

```python
import functools
import math

import jax
import jax.numpy as jnp
import ml_dtypes
import numpy as np
from jax import lax
from jax.experimental import pallas as pl
from jax.experimental.pallas import tpu as pltpu
from jax.sharding import PartitionSpec as P

NZ = 128
NX = 64
NY = 128
NSTICK = 3072
STATES = 16
PLANES = 8
CHUNK = NSTICK // PLANES
SPACING = 0.5
CELLS = NX * NY * NZ
NORM = 1.0 / math.sqrt(4.0 * NSTICK * NZ)
F32 = jnp.float32
BF16 = jnp.bfloat16
MESH = pl.DeviceIdType.MESH
VMEM_LIMIT = 60 * 1024 * 1024


def two_parts(table):
    high = np.asarray(table, np.float64).astype(ml_dtypes.bfloat16)
    low = (np.asarray(table, np.float64) - high.astype(np.float64)).astype(ml_dtypes.bfloat16)
    return np.stack([high, low])


def wave_table(out_freq, in_freq, count, sign):
    angle = 2.0 * np.pi * (np.outer(out_freq, in_freq) % count) / count
    cos, sin = np.cos(angle), sign * np.sin(angle)
    return np.block([[cos, -sin], [sin, cos]])


def derivative_matrix(count):
    signed = np.arange(count)
    signed = np.where(signed >= count // 2, signed - count, signed)
    deriv = np.where(signed == -(count // 2), 0, signed) * 2.0 * np.pi / (count * SPACING)
    return np.real(np.fft.ifft(1j * deriv[:, None] * np.fft.fft(np.eye(count), axis=0), axis=0))


def cas_matrix(count):
    angle = 2.0 * np.pi * (np.outer(np.arange(count), np.arange(count)) % count) / count
    return np.cos(angle) + np.sin(angle)


def squared_freq(count):
    signed = np.arange(count)
    signed = np.where(signed >= count // 2, signed - count, signed)
    return (signed * 2.0 * np.pi / (count * SPACING)) ** 2


@functools.cache
def tables():
    steps = np.arange(128)
    zwave = wave_table(steps, steps, NZ, 1.0).reshape(2, PLANES, 16, 256)
    zin = NORM * zwave.transpose(1, 0, 2, 3).reshape(256, 256)
    zwave = wave_table(steps, steps, NZ, -1.0).reshape(256, 2, PLANES, 16)
    zout = -zwave.transpose(0, 2, 1, 3).reshape(256, 256) / (CELLS * NORM)
    yin = wave_table(steps, steps, NY, 1.0).T
    yout = wave_table(steps, steps, NY, -1.0).T
    gx = np.concatenate([np.arange(0, NX, 2), np.arange(1, NX, 2)])
    xin = wave_table(np.arange(NX), gx, NX, 1.0)
    xout = wave_table(gx, np.arange(NX), NX, -1.0)
    dx, hx = derivative_matrix(NX), cas_matrix(NX)
    xmid = np.concatenate([dx.reshape(8, 8, NX), hx.reshape(8, 8, NX)], axis=1)
    dz = derivative_matrix(NZ)[:, 0]
    dz = np.concatenate([dz, dz, dz]).astype(np.float32)
    g_sq = squared_freq(NZ)[:, None, None] + squared_freq(NX)[None, :, None] + squared_freq(NY)[None, None, :]
    hart = np.where(g_sq > 0, 4.0 * np.pi / np.where(g_sq > 0, g_sq, 1.0), 0.0)
    along = np.real(np.fft.ifft(hart, axis=0))[: NZ // 2 + 1] / (NX * NY)
    along = along.reshape(65, 8, 8, NY).transpose(1, 0, 2, 3).astype(np.float32)
    return {
        "zin": two_parts(zin),
        "zout": two_parts(zout),
        "yin": two_parts(yin),
        "yout": two_parts(yout),
        "xin": two_parts(xin),
        "xout": two_parts(xout),
        "xmid": two_parts(xmid),
        "dy": two_parts(derivative_matrix(NY).T),
        "hy": two_parts(cas_matrix(NY)),
        "hx": two_parts(hx),
        "dz": dz,
        "along": along,
    }


def parts(values):
    high = values.astype(BF16)
    return high, (values - high.astype(F32)).astype(BF16)


def dot(a, b):
    return jnp.dot(a, b, preferred_element_type=F32)


def dot_t(a, b):
    return lax.dot_general(a, b, (((1,), (1,)), ((), ())), preferred_element_type=F32)


def table_first(table, values):
    high, low = parts(values)
    return dot(table[0], high) + dot(table[0], low) + dot(table[1], high)


def table_last(values, table):
    high, low = parts(values)
    return dot(high, table[0]) + dot(low, table[0]) + dot(high, table[1])


def meet(peers):
    barrier = pltpu.get_barrier_semaphore()
    for peer in peers:
        pl.semaphore_signal(barrier, inc=1, device_id=peer, device_id_type=MESH)
    return barrier


def exchange(src, dst, send_sem, recv_sem):
    me = lax.axis_index("plane")
    copies = []
    for step in range(1, PLANES):
        peer = lax.rem(me + step, PLANES)
        copy = pltpu.make_async_remote_copy(
            src_ref=src.at[peer],
            dst_ref=dst.at[me],
            send_sem=send_sem.at[step],
            recv_sem=recv_sem.at[step],
            device_id={"plane": peer},
            device_id_type=MESH,
        )
        copy.start()
        copies.append(copy)
    dst[me] = src[me]
    for copy in copies:
        copy.wait()


def sticks_kernel(coeffs, mask, zin, out, held, send_sem, recv_sem):
    me = lax.axis_index("plane")
    barrier = meet([{"plane": lax.rem(me + step, PLANES)} for step in range(1, PLANES)])
    keep = mask[...].astype(F32)
    values = (coeffs[...] * keep[None]).reshape(2 * NZ, CHUNK)
    held[...] = table_first(zin, values).reshape(PLANES, 32, CHUNK)
    pl.semaphore_wait(barrier, PLANES - 1)
    exchange(held, out, send_sem, recv_sem)


def back_kernel(picked, mask, zout, out, held, send_sem, recv_sem):
    me = lax.axis_index("plane")
    barrier = meet([{"plane": lax.rem(me + step, PLANES)} for step in range(1, PLANES)])
    pl.semaphore_wait(barrier, PLANES - 1)
    exchange(picked, held, send_sem, recv_sem)
    force = table_first(zout, held[...].reshape(256, CHUNK)).reshape(2, NZ, CHUNK)
    out[...] = force * mask[...].astype(F32)[None]


def one_hots(cols, chunk):
    col = cols[pl.ds(chunk, 1), :]
    upper, lower = col >> 8, col & 255
    rows = lax.broadcasted_iota(jnp.int32, (32, CHUNK), 0)
    above = jnp.where(rows == upper, 1.0, 0.0)
    rows = lax.broadcasted_iota(jnp.int32, (256, CHUNK), 0)
    below = jnp.where(rows == lower, 1.0, 0.0).astype(BF16)
    return above, below


def wave_kernel(sticks, cols, yin, xin, psi, density, grid, lines):
    for chunk in range(PLANES):
        above, below = one_hots(cols, chunk)
        above = above.astype(BF16)[None]
        high, low = parts(sticks[chunk])
        left = (high[:, None, :] * above).reshape(1024, CHUNK)
        total = dot_t(left, below)
        left = (low[:, None, :] * above).reshape(1024, CHUNK)
        total = total + dot_t(left, below)
        if chunk == 0:
            grid[...] = total
        else:
            grid[...] += total
    for odd in range(2):
        lanes = slice(odd * 128, odd * 128 + 128)
        rows = jnp.concatenate([grid[0:512, lanes], grid[512:1024, lanes]], axis=1)
        turned = table_last(rows, yin)
        for z in range(16):
            for c in range(2):
                first = c * 64 + odd * 32
                lines[first : first + 32, z * 128 : z * 128 + 128] = turned[
                    z * 32 : z * 32 + 32, c * 128 : c * 128 + 128
                ]
    wave = table_first(xin, lines[...])
    psi[...] = wave
    density[...] = (wave[:64] * wave[:64] + wave[64:] * wave[64:]) * (1.0 / STATES)


def force_kernel(psi, near, far, cols, hx, hy, xout, yout, picked, lines, grid):
    turned = table_first(hx, far[...])
    rows = jnp.concatenate([turned[:, z * 128 : z * 128 + 128] for z in range(16)], axis=0)
    turned = table_last(rows, hy)
    for z in range(16):
        lanes = slice(z * 128, z * 128 + 128)
        potential = near[:, lanes] + turned[z * 64 : z * 64 + 64]
        lines[0:64, lanes] = potential * psi[0:64, lanes]
        lines[64:128, lanes] = potential * psi[64:128, lanes]
    lines[...] = table_first(xout, lines[...])
    for odd in range(2):
        rows = jnp.concatenate(
            [
                jnp.concatenate(
                    [
                        lines[c * 64 + odd * 32 : c * 64 + odd * 32 + 32, z * 128 : z * 128 + 128]
                        for z in range(16)
                    ],
                    axis=0,
                )
                for c in range(2)
            ],
            axis=1,
        )
        turned = table_last(rows, yout)
        lanes = slice(odd * 128, odd * 128 + 128)
        grid[0:512, lanes] = turned[:, 0:128]
        grid[512:1024, lanes] = turned[:, 128:256]
    high, low = parts(grid[...])
    for chunk in range(PLANES):
        above, below = one_hots(cols, chunk)
        total = dot(high, below) + dot(low, below)
        picked[chunk] = jnp.sum(total.reshape(32, 32, CHUNK) * above[None], axis=1)


def xc_terms(rho, g):
    kappa, mu = 0.804, 0.2195
    exch = 0.75 * (3.0 / math.pi) ** (1.0 / 3.0)
    scale = 1.0 / (4.0 * (3.0 * math.pi**2) ** (2.0 / 3.0))
    root = jnp.exp(jnp.log(rho) * (1.0 / 3.0))
    root = root - (root * root * root - rho) / (3.0 * root * root)
    four = rho * root
    s2 = scale * g / (four * four)
    q = 1.0 / (1.0 + s2 * (mu / kappa))
    enhance = 1.0 + kappa - kappa * q
    radius = (3.0 / (4.0 * math.pi)) ** (1.0 / 3.0) / root
    inverse = 1.0 / (7.8 + radius)
    v_local = -exch * root * ((4.0 / 3.0) * enhance - (8.0 / 3.0) * mu * s2 * q * q)
    v_local = v_local - 0.44 * inverse - (0.44 / 3.0) * radius * inverse * inverse
    return v_local, (-2.0 * exch * mu * scale) * q * q / four


def tiles(block):
    return jnp.concatenate([block[:, z * 128 : z * 128 + 128] for z in range(8)], axis=0)


def untile(rows):
    return jnp.concatenate([rows[z * 8 : z * 8 + 8] for z in range(8)], axis=1)


def along_z(source, home, weight):
    def body(other, sums):
        base = home - other * 8 + 128
        held = [source[other, :, z * 128 : z * 128 + 128] for z in range(8)]
        factors = {shift: weight(base + shift) for shift in range(-7, 8)}
        sums = list(sums)
        for to in range(8):
            for z in range(8):
                sums[to] = sums[to] + factors[to - z] * held[z]
        return tuple(sums)

    sums = lax.fori_loop(0, 16, body, tuple(jnp.zeros((8, 128), F32) for _ in range(8)))
    return jnp.concatenate(sums, axis=1)


def middle_kernel(
    partial, core, xmid, dy, hy, dz, along, near, far,
    given, block, flux_x, flux_z, rho_hat, near_own, far_own, by_x, by_x2, by_z, by_z2, by_z3, kernel_z,
    kernel_sem, send, recv,
):
    s, p = lax.axis_index("state"), lax.axis_index("plane")
    band, half = s // 2, lax.rem(s, 2)
    place = p * 2 + half

    fetch = pltpu.make_async_copy(along.at[band], kernel_z, kernel_sem)
    fetch.start()

    states = [lax.rem(s + step, 16) for step in range(1, 16)]
    bands = [lax.rem(band + step, 8) * 2 + half for step in range(1, 8)]
    places = [lax.rem(place + step, 16) for step in range(1, 16)]
    places = [{"state": band * 2 + lax.rem(other, 2), "plane": other // 2} for other in places]

    barrier = meet(
        [{"state": other, "plane": p} for other in states]
        + [
            {"state": band * 2 + part, "plane": lax.rem(p + step, 8)}
            for step in range(1, 8)
            for part in range(2)
        ]
    )
    pl.semaphore_wait(barrier, 29)

    count = [0]

    def post(src, dst, to):
        at = count[0]
        count[0] += 1
        copy = pltpu.make_async_remote_copy(
            src_ref=src, dst_ref=dst, send_sem=send.at[at], recv_sem=recv.at[at], device_id=to, device_id_type=MESH
        )
        copy.start()
        return copy

    def rows_of(other):
        return pl.ds(pl.multiple_of(other // 2 * 8, 8), 8)

    def lanes_of(other):
        return pl.ds(pl.multiple_of(lax.rem(other, 2) * 1024, 1024), 1024)

    copies = [
        post(partial.at[rows_of(other), lanes_of(other)], given.at[s], {"state": other, "plane": p})
        for other in states
    ]
    own = [core[half * 8 + z, rows_of(s), :] for z in range(8)]
    rho = jnp.concatenate(own, axis=1) + partial[rows_of(s), lanes_of(s)]
    for copy, other in zip(copies, range(1, 16)):
        copy.wait()
        rho = rho + given[lax.rem(s - other + 16, 16)]
    block[...] = rho

    def all_x(src, dst):
        return [post(src, dst.at[rows_of(s), :], {"state": other, "plane": p}) for other in bands]

    def all_z(src, dst):
        return [post(src, dst.at[place], to) for to in places]

    def done(copies):
        for copy in copies:
            copy.wait()

    x_copies, z_copies = all_x(block, by_x), all_z(block, by_z)
    by_x[rows_of(s), :] = rho
    by_z[place] = rho
    rows = tiles(rho)
    grad_y = untile(table_last(rows, dy))
    done(x_copies)
    high, low = parts(by_x[...])
    both = dot(xmid[0, band], high) + dot(xmid[0, band], low) + dot(xmid[1, band], high)
    grad_x, rho_x = both[:8], both[8:]
    rho_xy = untile(table_last(tiles(rho_x), hy))
    rho_hat[...] = rho_xy
    r_copies = all_z(rho_hat, by_z3)
    by_z3[place] = rho_xy
    done(z_copies)
    home = place * 8
    grad_z = along_z(by_z, home, lambda at: dz[at])
    v_local, twice = xc_terms(rho, grad_z * grad_z + grad_x * grad_x + grad_y * grad_y)
    flux = twice * grad_z
    flux_z[...] = flux
    z_copies = all_z(flux_z, by_z2)
    by_z2[place] = flux
    flux = twice * grad_x
    flux_x[...] = flux
    x_copies = all_x(flux_x, by_x2)
    by_x2[rows_of(s), :] = flux
    total = v_local - untile(table_last(tiles(twice * grad_y), dy))

    fetch.wait()
    done(r_copies)

    def weight(at):
        at = lax.rem(at, 128)
        return kernel_z[jnp.minimum(at, 128 - at)]

    spread = along_z(by_z3, home, weight)
    far_own[...] = spread

    def all_states(src, dst):
        return [
            post(src, dst.at[rows_of(s), lanes_of(s)], {"state": other, "plane": p}) for other in states
        ]

    f_copies = all_states(far_own, far)
    far[rows_of(s), lanes_of(s)] = spread
    done(x_copies)
    high, low = parts(by_x2[...])
    both = dot(xmid[0, band], high) + dot(xmid[0, band], low) + dot(xmid[1, band], high)
    total = total - both[:8]
    done(z_copies)
    total = total - along_z(by_z2, home, lambda at: dz[at])
    near_own[...] = total
    n_copies = all_states(near_own, near)
    near[rows_of(s), lanes_of(s)] = total
    done(f_copies)
    done(n_copies)


VM = pl.BlockSpec(memory_space=pltpu.VMEM)


def call(kernel, outs, ins, scratch, in_specs=None, collective=None):
    return pl.pallas_call(
        kernel,
        out_shape=[jax.ShapeDtypeStruct(shape, F32) for shape in outs],
        in_specs=in_specs or [VM] * len(ins),
        out_specs=[VM] * len(outs),
        scratch_shapes=scratch,
        compiler_params=pltpu.CompilerParams(
            collective_id=collective,
            has_side_effects=collective is not None,
            vmem_limit_bytes=VMEM_LIMIT,
        ),
    )(*ins)


def on_device(coeffs, mask, stick_cols, core):
    t = {name: jnp.asarray(table) for name, table in tables().items()}
    cols = stick_cols.reshape(PLANES, CHUNK)
    sems = [pltpu.SemaphoreType.DMA((PLANES,))] * 2
    sticks, = call(
        sticks_kernel,
        [(PLANES, 32, CHUNK)],
        [coeffs.reshape(2, NZ, CHUNK), mask, t["zin"]],
        [pltpu.VMEM((PLANES, 32, CHUNK), F32), *sems],
        collective=0,
    )
    psi, partial = call(
        wave_kernel,
        [(128, 2048), (64, 2048)],
        [sticks, cols, t["yin"], t["xin"]],
        [pltpu.VMEM((1024, 256), F32), pltpu.VMEM((128, 2048), F32)],
    )
    own = pltpu.VMEM((8, 1024), F32)
    near, far = call(
        middle_kernel,
        [(64, 2048), (64, 2048)],
        [partial, core, t["xmid"], t["dy"], t["hy"], t["dz"], t["along"]],
        [
            pltpu.VMEM((16, 8, 1024), F32), own, own, own, own, own, own,
            pltpu.VMEM((64, 1024), F32), pltpu.VMEM((64, 1024), F32),
            pltpu.VMEM((16, 8, 1024), F32), pltpu.VMEM((16, 8, 1024), F32), pltpu.VMEM((16, 8, 1024), F32),
            pltpu.VMEM((65, 8, 128), F32),
            pltpu.SemaphoreType.DMA,
            pltpu.SemaphoreType.DMA((104,)),
            pltpu.SemaphoreType.DMA((104,)),
        ],
        in_specs=[VM] * 5 + [pl.BlockSpec(memory_space=pltpu.SMEM), pl.BlockSpec(memory_space=pl.ANY)],
        collective=1,
    )
    picked, = call(
        force_kernel,
        [(PLANES, 32, CHUNK)],
        [psi, near, far, cols, t["hx"], t["hy"], t["xout"], t["yout"]],
        [pltpu.VMEM((128, 2048), F32), pltpu.VMEM((1024, 256), F32)],
    )
    forces, = call(
        back_kernel,
        [(2, NZ, CHUNK)],
        [picked, mask, t["zout"]],
        [pltpu.VMEM((PLANES, 32, CHUNK), F32), *sems],
        collective=2,
    )
    return forces.reshape(2, 1, NZ, CHUNK)


def solution(mesh):
    in_specs = (P(None, "state", None, "plane"), P(None, "plane"), P(), P("plane", None, None))
    out_specs = P(None, "state", None, "plane")
    return jax.shard_map(
        on_device, mesh=mesh, in_specs=in_specs, out_specs=out_specs, check_vma=False
    )
```

```python
import functools
import math

import jax
import jax.numpy as jnp
import ml_dtypes
import numpy as np
from jax import lax
from jax.experimental import pallas as pl
from jax.experimental.pallas import tpu as pltpu
from jax.sharding import PartitionSpec as P

NZ = 128
NX = 64
NY = 128
NSTICK = 3072
STATES = 16
PLANES = 8
CHUNK = NSTICK // PLANES
SPACING = 0.5
CELLS = NX * NY * NZ
NORM = 1.0 / math.sqrt(4.0 * NSTICK * NZ)
F32 = jnp.float32
BF16 = jnp.bfloat16
MESH = pl.DeviceIdType.MESH
VMEM_LIMIT = 60 * 1024 * 1024


def two_parts(table):
    high = np.asarray(table, np.float64).astype(ml_dtypes.bfloat16)
    low = (np.asarray(table, np.float64) - high.astype(np.float64)).astype(ml_dtypes.bfloat16)
    return np.stack([high, low])


def wave_table(out_freq, in_freq, count, sign):
    angle = 2.0 * np.pi * (np.outer(out_freq, in_freq) % count) / count
    cos, sin = np.cos(angle), sign * np.sin(angle)
    return np.block([[cos, -sin], [sin, cos]])


def derivative_matrix(count):
    signed = np.arange(count)
    signed = np.where(signed >= count // 2, signed - count, signed)
    deriv = np.where(signed == -(count // 2), 0, signed) * 2.0 * np.pi / (count * SPACING)
    return np.real(np.fft.ifft(1j * deriv[:, None] * np.fft.fft(np.eye(count), axis=0), axis=0))


def cas_matrix(count):
    angle = 2.0 * np.pi * (np.outer(np.arange(count), np.arange(count)) % count) / count
    return np.cos(angle) + np.sin(angle)


def squared_freq(count):
    signed = np.arange(count)
    signed = np.where(signed >= count // 2, signed - count, signed)
    return (signed * 2.0 * np.pi / (count * SPACING)) ** 2


@functools.cache
def tables():
    steps = np.arange(128)
    zwave = wave_table(steps, steps, NZ, 1.0).reshape(2, PLANES, 16, 256)
    zin = NORM * zwave.transpose(1, 0, 2, 3).reshape(256, 256)
    zwave = wave_table(steps, steps, NZ, -1.0).reshape(256, 2, PLANES, 16)
    zout = -zwave.transpose(0, 2, 1, 3).reshape(256, 256) / (CELLS * NORM)
    yin = wave_table(steps, steps, NY, 1.0).T
    yout = wave_table(steps, steps, NY, -1.0).T
    gx = np.concatenate([np.arange(0, NX, 2), np.arange(1, NX, 2)])
    xin = wave_table(np.arange(NX), gx, NX, 1.0)
    xout = wave_table(gx, np.arange(NX), NX, -1.0)
    dx, hx = derivative_matrix(NX), cas_matrix(NX)
    xmid = np.concatenate([dx.reshape(8, 8, NX), hx.reshape(8, 8, NX)], axis=1)
    dz = derivative_matrix(NZ)[:, 0]
    dz = np.concatenate([dz, dz, dz]).astype(np.float32)
    g_sq = squared_freq(NZ)[:, None, None] + squared_freq(NX)[None, :, None] + squared_freq(NY)[None, None, :]
    hart = np.where(g_sq > 0, 4.0 * np.pi / np.where(g_sq > 0, g_sq, 1.0), 0.0)
    along = np.real(np.fft.ifft(hart, axis=0))[: NZ // 2 + 1] / (NX * NY)
    along = along.reshape(65, 8, 8, NY).transpose(1, 0, 2, 3).astype(np.float32)
    return {
        "zin": two_parts(zin),
        "zout": two_parts(zout),
        "yin": two_parts(yin),
        "yout": two_parts(yout),
        "xin": two_parts(xin),
        "xout": two_parts(xout),
        "xmid": two_parts(xmid),
        "dy": two_parts(derivative_matrix(NY).T),
        "hy": two_parts(cas_matrix(NY)),
        "hx": two_parts(hx),
        "dz": dz,
        "along": along,
    }


def parts(values):
    high = values.astype(BF16)
    return high, (values - high.astype(F32)).astype(BF16)


def dot(a, b):
    return jnp.dot(a, b, preferred_element_type=F32)


def dot_t(a, b):
    return lax.dot_general(a, b, (((1,), (1,)), ((), ())), preferred_element_type=F32)


def table_first(table, values):
    high, low = parts(values)
    return dot(table[0], high) + dot(table[0], low) + dot(table[1], high)


def table_last(values, table):
    high, low = parts(values)
    return dot(high, table[0]) + dot(low, table[0]) + dot(high, table[1])


def one_hot(values, rows):
    places = lax.broadcasted_iota(jnp.int32, (rows, values.shape[1]), 0)
    return jnp.where(places == values, 1.0, 0.0)


def columns_of(cols, chunk):
    return cols[:, pl.ds(pl.multiple_of(chunk * CHUNK, 128), CHUNK)]


def xc_terms(rho, g):
    kappa, mu = 0.804, 0.2195
    exch = 0.75 * (3.0 / math.pi) ** (1.0 / 3.0)
    scale = 1.0 / (4.0 * (3.0 * math.pi**2) ** (2.0 / 3.0))
    root = jnp.exp(jnp.log(rho) * (1.0 / 3.0))
    root = root - (root * root * root - rho) / (3.0 * root * root)
    four = rho * root
    s2 = scale * g / (four * four)
    q = 1.0 / (1.0 + s2 * (mu / kappa))
    enhance = 1.0 + kappa - kappa * q
    radius = (3.0 / (4.0 * math.pi)) ** (1.0 / 3.0) / root
    inverse = 1.0 / (7.8 + radius)
    v_local = -exch * root * ((4.0 / 3.0) * enhance - (8.0 / 3.0) * mu * s2 * q * q)
    v_local = v_local - 0.44 * inverse - (0.44 / 3.0) * radius * inverse * inverse
    return v_local, (-2.0 * exch * mu * scale) * q * q / four


def tiles(block, count):
    return jnp.concatenate([block[:, z * 128 : z * 128 + 128] for z in range(8)], axis=0)


def untile(rows, count):
    return jnp.concatenate([rows[z * count : z * count + count] for z in range(8)], axis=1)


def along_z(source, base, weight):
    def body(other, sums):
        start = base - other * 16
        held = [source[other, :, z * 128 : z * 128 + 128] for z in range(8)]
        factors = {shift: weight(start + shift) for shift in range(-7, 8)}
        sums = list(sums)
        for to in range(8):
            for z in range(8):
                sums[to] = sums[to] + factors[to - z] * held[z]
        return tuple(sums)

    sums = lax.fori_loop(0, PLANES, body, tuple(jnp.zeros((8, 128), F32) for _ in range(8)))
    return jnp.concatenate(sums, axis=1)


STEPS = ((2, 1), (1, 1), (3, 1), (2, 0), (0, 1), (1, 0), (3, 0))


def partner(place, ring, pair):
    return lax.rem(place // 2 + ring, 4) * 2 + lax.rem(place + pair, 2)


def step_kernel(
    coeffs, mask, cols, core, zin, yin, xin, xmid, dy, hy, hx, xout, yout, dz, along,
    back,
    held, sticks, grid, lines, psi, partial, summed, given,
    block, flux_x, flux_z, rho_hat, near_own, far_own, to_twin, from_twin,
    by_x, by_x2, by_z, by_z2, by_z3, kernel_z, near, far, pot, pot_twin, picked,
    kernel_sem, send, recv,
):
    s, p = lax.axis_index("state"), lax.axis_index("plane")
    band, half = s // 2, lax.rem(s, 2)
    twin = 1 - half

    fetch = pltpu.make_async_copy(along.at[band], kernel_z, kernel_sem)
    fetch.start()

    def on_plane(ring, pair):
        return {"state": s, "plane": partner(p, ring, pair)}

    def on_band(ring, pair):
        return {"state": partner(band, ring, pair) * 2 + half, "plane": p}

    on_twin = {"state": band * 2 + twin, "plane": p}

    barrier = pltpu.get_barrier_semaphore()
    for to in [on_twin] + [on_plane(*step) for step in STEPS] + [on_band(*step) for step in STEPS]:
        pl.semaphore_signal(barrier, inc=1, device_id=to, device_id_type=MESH)

    count = [0]

    def post(src, dst, to):
        at = count[0]
        count[0] += 1
        copy = pltpu.make_async_remote_copy(
            src_ref=src, dst_ref=dst, send_sem=send.at[at], recv_sem=recv.at[at], device_id=to, device_id_type=MESH
        )
        copy.start()
        return copy

    def done(copies):
        for copy in copies:
            copy.wait()

    def rows_of(other):
        return pl.ds(pl.multiple_of(other * 8, 8), 8)

    def lanes_of(part):
        return pl.ds(pl.multiple_of(part * 1024, 1024), 1024)

    values = (coeffs[...] * mask[...].astype(F32)[None]).reshape(2 * NZ, CHUNK)
    held[...] = table_first(zin, values).reshape(PLANES, 32, CHUNK)
    pl.semaphore_wait(barrier, 15)
    copies = [post(held.at[partner(p, *step)], sticks.at[p], on_plane(*step)) for step in STEPS]
    sticks[p] = held[p]

    def place(chunk):
        col = columns_of(cols, chunk)
        above = one_hot(col >> 8, 32).astype(BF16)[None]
        below = one_hot(col & 255, 256).astype(BF16)
        high, low = parts(sticks[chunk])
        left = jnp.concatenate(
            [(part[:, None, :] * above).reshape(1024, CHUNK) for part in (high, low)], axis=1
        )
        return dot_t(left, jnp.concatenate([below, below], axis=1))

    grid[...] = place(p)
    for copy, (ring, pair) in reversed(list(zip(copies, STEPS))):
        copy.wait()
        grid[...] += place(partner(p, 4 - ring, pair))

    for odd in range(2):
        lanes = slice(odd * 128, odd * 128 + 128)
        rows = jnp.concatenate([grid[0:512, lanes], grid[512:1024, lanes]], axis=1)
        turned = table_last(rows, yin)
        for z in range(16):
            for c in range(2):
                first = c * 64 + odd * 32
                lines[first : first + 32, z * 128 : z * 128 + 128] = turned[
                    z * 32 : z * 32 + 32, c * 128 : c * 128 + 128
                ]

    def waves(part):
        wave = table_first(xin, lines[:, lanes_of(part)])
        psi[:, lanes_of(part)] = wave
        return (wave[:64] * wave[:64] + wave[64:] * wave[64:]) * (1.0 / STATES)

    to_twin[...] = waves(twin)
    copy = post(to_twin, from_twin, on_twin)
    own = waves(half)
    copy.wait()
    summed[...] = own + from_twin[...]

    copies = [post(summed.at[rows_of(partner(band, *step)), :], given.at[band], on_band(*step)) for step in STEPS]
    rho = jnp.concatenate([core[half * 8 + z, rows_of(band), :] for z in range(8)], axis=1)
    rho = rho + summed[rows_of(band), :]
    for copy, (ring, pair) in reversed(list(zip(copies, STEPS))):
        copy.wait()
        rho = rho + given[partner(band, 4 - ring, pair)]
    block[...] = rho

    def all_bands(src, dst):
        return [post(src, dst.at[rows_of(band), :], on_band(*step)) for step in STEPS]

    def all_planes(src, dst):
        return [post(src, dst.at[p], on_plane(*step)) for step in STEPS]

    def across(source, weight, slot):
        base = p * 16 + 128
        partial[slot, 0] = along_z(source, base + (twin - half) * 8, weight)
        copy = post(partial.at[slot, 0], partial.at[slot, 1], on_twin)
        total = along_z(source, base, weight)
        copy.wait()
        return total + partial[slot, 1]

    def slope(at):
        return dz[at]

    def mixed_x(source):
        high, low = parts(source[...])
        return dot(xmid[0, band], high) + dot(xmid[0, band], low) + dot(xmid[1, band], high)

    x_copies, z_copies = all_bands(block, by_x), all_planes(block, by_z)
    by_x[rows_of(band), :] = rho
    by_z[p] = rho
    grad_y = untile(table_last(tiles(rho, 8), dy), 8)
    done(x_copies)
    both = mixed_x(by_x)
    grad_x = both[:8]
    rho_xy = untile(table_last(tiles(both[8:], 8), hy), 8)
    rho_hat[...] = rho_xy
    r_copies = all_planes(rho_hat, by_z3)
    by_z3[p] = rho_xy
    done(z_copies)
    grad_z = across(by_z, slope, 0)

    v_local, twice = xc_terms(rho, grad_z * grad_z + grad_x * grad_x + grad_y * grad_y)
    flux = twice * grad_z
    flux_z[...] = flux
    z_copies = all_planes(flux_z, by_z2)
    by_z2[p] = flux
    flux = twice * grad_x
    flux_x[...] = flux
    x_copies = all_bands(flux_x, by_x2)
    by_x2[rows_of(band), :] = flux
    total = v_local - untile(table_last(tiles(twice * grad_y, 8), dy), 8)

    fetch.wait()
    done(r_copies)

    def even(at):
        at = lax.rem(at, 128)
        return kernel_z[jnp.minimum(at, 128 - at)]

    spread = across(by_z3, even, 1)
    far_own[...] = spread
    f_copies = all_bands(far_own, far)
    far[rows_of(band), :] = spread

    done(x_copies)
    total = total - mixed_x(by_x2)[:8]
    done(z_copies)
    total = total - across(by_z2, slope, 2)
    near_own[...] = total
    n_copies = all_bands(near_own, near)
    near[rows_of(band), :] = total

    done(f_copies)
    turned = untile(table_last(tiles(table_first(hx, far[...]), 64), hy), 64)
    done(n_copies)
    pot[...] = near[...] + turned
    copy = post(pot, pot_twin, on_twin)

    def forces(potential, part):
        lanes = lanes_of(part)
        wave = psi[:, lanes]
        wave = jnp.concatenate([potential * wave[:64], potential * wave[64:]], axis=0)
        wave = table_first(xout, wave)
        for odd in range(2):
            rows = []
            for c in range(2):
                first = c * 64 + odd * 32
                rows.append(
                    jnp.concatenate([wave[first : first + 32, z * 128 : z * 128 + 128] for z in range(8)], axis=0)
                )
            turned = table_last(jnp.concatenate(rows, axis=1), yout)
            for c in range(2):
                at = pl.ds(pl.multiple_of(c * 512 + part * 256, 256), 256)
                grid[at, odd * 128 : odd * 128 + 128] = turned[:, c * 128 : c * 128 + 128]

    forces(pot[...], half)
    copy.wait()
    forces(pot_twin[...], twin)

    high, low = parts(grid[...])
    left = jnp.concatenate([high, low], axis=1)
    copies = []
    order = STEPS + ((0, 0),)
    for first in range(0, PLANES, 2):
        steps = order[first : first + 2]
        owners = [partner(p, *step) for step in steps]
        col = jnp.concatenate([columns_of(cols, owner) for owner in owners], axis=1)
        above = one_hot(col >> 8, 32)[None]
        below = one_hot(col & 255, 256).astype(BF16)
        found = dot(left, jnp.concatenate([below, below], axis=0)).reshape(32, 32, 2 * CHUNK)
        found = jnp.sum(found * above, axis=1)
        for at, (step, owner) in enumerate(zip(steps, owners)):
            chunk = found[:, at * CHUNK : (at + 1) * CHUNK]
            if step == (0, 0):
                back[p] = chunk
            else:
                picked[owner] = chunk
                copies.append(post(picked.at[owner], back.at[p], on_plane(*step)))
    done(copies)


def last_kernel(back, mask, zout, out):
    force = table_first(zout, back[...].reshape(256, CHUNK)).reshape(2, NZ, CHUNK)
    out[...] = force * mask[...].astype(F32)[None]


VM = pl.BlockSpec(memory_space=pltpu.VMEM)
COPIES = 7 * 10 + 5


def call(kernel, outs, ins, scratch=(), in_specs=None, collective=None):
    return pl.pallas_call(
        kernel,
        out_shape=[jax.ShapeDtypeStruct(shape, F32) for shape in outs],
        in_specs=in_specs or [VM] * len(ins),
        out_specs=[VM] * len(outs),
        scratch_shapes=scratch,
        compiler_params=pltpu.CompilerParams(
            collective_id=collective,
            has_side_effects=collective is not None,
            vmem_limit_bytes=VMEM_LIMIT,
        ),
    )(*ins)


def on_device(coeffs, mask, stick_cols, core):
    t = {name: jnp.asarray(table) for name, table in tables().items()}
    names = ("zin", "yin", "xin", "xmid", "dy", "hy", "hx", "xout", "yout")
    bundle, own, all_x, all_z = (PLANES, 32, CHUNK), (8, 1024), (64, 1024), (PLANES, 8, 1024)
    shapes = [bundle, bundle, (1024, 256), (128, 2048), (128, 2048), (3, 2, 8, 1024), all_x, all_z]
    shapes += [own] * 6 + [all_x] * 2
    shapes += [all_x] * 2 + [all_z] * 3 + [(65, 8, 128)] + [all_x] * 4 + [bundle]
    back, = call(
        step_kernel,
        [bundle],
        [coeffs.reshape(2, NZ, CHUNK), mask, stick_cols.reshape(1, NSTICK), core]
        + [t[name] for name in names]
        + [t["dz"], t["along"]],
        [pltpu.VMEM(shape, F32) for shape in shapes]
        + [pltpu.SemaphoreType.DMA, pltpu.SemaphoreType.DMA((COPIES,)), pltpu.SemaphoreType.DMA((COPIES,))],
        in_specs=[VM] * 13 + [pl.BlockSpec(memory_space=pltpu.SMEM), pl.BlockSpec(memory_space=pl.ANY)],
        collective=0,
    )
    forces, = call(last_kernel, [(2, NZ, CHUNK)], [back, mask, t["zout"]])
    return forces.reshape(2, 1, NZ, CHUNK)


def solution(mesh):
    in_specs = (P(None, "state", None, "plane"), P(None, "plane"), P(), P("plane", None, None))
    out_specs = P(None, "state", None, "plane")
    return jax.shard_map(
        on_device, mesh=mesh, in_specs=in_specs, out_specs=out_specs, check_vma=False
    )
```

```python
import functools
import math

import jax
import jax.numpy as jnp
import ml_dtypes
import numpy as np
from jax import lax
from jax.experimental import pallas as pl
from jax.experimental.pallas import tpu as pltpu
from jax.sharding import PartitionSpec as P

NZ = 128
NX = 64
NY = 128
NSTICK = 3072
STATES = 16
PLANES = 8
CHUNK = NSTICK // PLANES
SPACING = 0.5
CELLS = NX * NY * NZ
NORM = 1.0 / math.sqrt(4.0 * NSTICK * NZ)
F32 = jnp.float32
BF16 = jnp.bfloat16
MESH = pl.DeviceIdType.MESH


def two_parts(table):
    high = np.asarray(table, np.float64).astype(ml_dtypes.bfloat16)
    low = (np.asarray(table, np.float64) - high.astype(np.float64)).astype(ml_dtypes.bfloat16)
    return np.stack([high, low])


def wave_table(out_freq, in_freq, count, sign):
    angle = 2.0 * np.pi * (np.outer(out_freq, in_freq) % count) / count
    cos, sin = np.cos(angle), sign * np.sin(angle)
    return np.block([[cos, -sin], [sin, cos]])


def derivative_matrix(count):
    signed = np.arange(count)
    signed = np.where(signed >= count // 2, signed - count, signed)
    deriv = np.where(signed == -(count // 2), 0, signed) * 2.0 * np.pi / (count * SPACING)
    return np.real(np.fft.ifft(1j * deriv[:, None] * np.fft.fft(np.eye(count), axis=0), axis=0))


def cas_matrix(count):
    angle = 2.0 * np.pi * (np.outer(np.arange(count), np.arange(count)) % count) / count
    return np.cos(angle) + np.sin(angle)


def squared_freq(count):
    signed = np.arange(count)
    signed = np.where(signed >= count // 2, signed - count, signed)
    return (signed * 2.0 * np.pi / (count * SPACING)) ** 2


def four_parts(table):
    high, low = two_parts(table)
    return np.block([[high, high], [low, low]])


@functools.cache
def tables():
    steps = np.arange(128)
    zwave = wave_table(steps, steps, NZ, 1.0).reshape(2, PLANES, 16, 256)
    zin = NORM * zwave.transpose(1, 0, 2, 3).reshape(256, 256)
    zwave = wave_table(steps, steps, NZ, -1.0).reshape(256, 2, PLANES, 16)
    zout = -zwave.transpose(0, 2, 1, 3).reshape(256, 256) / (CELLS * NORM)
    yin = wave_table(steps, steps, NY, 1.0).T
    yout = wave_table(steps, steps, NY, -1.0).T
    gx = np.concatenate([np.arange(0, NX, 2), np.arange(1, NX, 2)])
    xin = wave_table(np.arange(NX), gx, NX, 1.0)
    xout = wave_table(gx, np.arange(NX), NX, -1.0)
    dx, hx = derivative_matrix(NX), cas_matrix(NX)
    xmid = np.concatenate([dx.reshape(8, 8, NX), hx.reshape(8, 8, NX)], axis=1)
    dz = derivative_matrix(NZ)[:, 0]
    dz = np.concatenate([dz, dz, dz]).astype(np.float32)
    g_sq = squared_freq(NZ)[:, None, None] + squared_freq(NX)[None, :, None] + squared_freq(NY)[None, None, :]
    hart = np.where(g_sq > 0, 4.0 * np.pi / np.where(g_sq > 0, g_sq, 1.0), 0.0)
    along = np.real(np.fft.ifft(hart, axis=0))[: NZ // 2 + 1] / (NX * NY)
    along = along.reshape(65, 8, 8, NY).transpose(1, 0, 2, 3).astype(np.float32)
    return {
        "zin": two_parts(zin),
        "zout": two_parts(zout),
        "yin": two_parts(yin),
        "yout": two_parts(yout),
        "xin": four_parts(xin),
        "xout": four_parts(xout),
        "xmid": two_parts(xmid),
        "dy": two_parts(derivative_matrix(NY).T),
        "hy": two_parts(cas_matrix(NY)),
        "hx": four_parts(hx),
        "dz": dz,
        "along": along,
    }


def parts(values):
    high = values.astype(BF16)
    return high, (values - high.astype(F32)).astype(BF16)


def dot(a, b):
    return jnp.dot(a, b, preferred_element_type=F32)


def dot_t(a, b):
    return lax.dot_general(a, b, (((1,), (1,)), ((), ())), preferred_element_type=F32)


def table_first(table, values):
    high, low = parts(values)
    return dot(table[0], high) + dot(table[0], low) + dot(table[1], high)


def four_first(table, values):
    both = dot(table[...], jnp.concatenate(parts(values), axis=0))
    half = table.shape[0] // 2
    return both[:half] + both[half:]


def table_last(values, table):
    high, low = parts(values)
    return dot(high, table[0]) + dot(low, table[0]) + dot(high, table[1])


def one_hot(values, rows):
    places = lax.broadcasted_iota(jnp.int32, (rows, values.shape[1]), 0)
    return jnp.where(places == values, 1.0, 0.0)


def columns_of(cols, chunk):
    return cols[:, pl.ds(pl.multiple_of(chunk * CHUNK, 128), CHUNK)]


def xc_terms(rho, g):
    kappa, mu = 0.804, 0.2195
    exch = 0.75 * (3.0 / math.pi) ** (1.0 / 3.0)
    scale = 1.0 / (4.0 * (3.0 * math.pi**2) ** (2.0 / 3.0))
    root = jnp.exp(jnp.log(rho) * (1.0 / 3.0))
    root = root - (root * root * root - rho) / (3.0 * root * root)
    four = rho * root
    s2 = scale * g / (four * four)
    q = 1.0 / (1.0 + s2 * (mu / kappa))
    enhance = 1.0 + kappa - kappa * q
    radius = (3.0 / (4.0 * math.pi)) ** (1.0 / 3.0) / root
    inverse = 1.0 / (7.8 + radius)
    v_local = -exch * root * ((4.0 / 3.0) * enhance - (8.0 / 3.0) * mu * s2 * q * q)
    v_local = v_local - 0.44 * inverse - (0.44 / 3.0) * radius * inverse * inverse
    return v_local, (-2.0 * exch * mu * scale) * q * q / four


def tiles(block, count):
    return jnp.concatenate([block[:, z * 128 : z * 128 + 128] for z in range(8)], axis=0)


def untile(rows, count):
    return jnp.concatenate([rows[z * count : z * count + count] for z in range(8)], axis=1)


STEPS = ((2, 1), (1, 1), (3, 1), (2, 0), (0, 1), (1, 0), (3, 0))


def partner(place, ring, pair):
    return lax.rem(place // 2 + ring, 4) * 2 + lax.rem(place + pair, 2)


FIRST = ("coeffs", "mask", "zin")
LOADED = FIRST + ("cols", "dz", "yin", "xin", "core", "xmid", "dy", "hy", "hx", "xout", "yout")


def step_kernel(along, *refs):
    away, (back, *refs) = refs[: len(LOADED)], refs[len(LOADED) :]
    work(along, away, back, refs[: len(LOADED)], *refs[len(LOADED) :])


def work(
    along, away, back, near_by,
    held, sticks, grid, psi, partial, summed, given,
    block, flux_x, flux_z, rho_hat, near_own, far_own, to_twin, from_twin,
    by_x, by_x2, by_z, by_z2, by_z3, kernel_z, near, far, pot, pot_twin, picked,
    kernel_sem, load_sem, send, recv,
):
    s, p = lax.axis_index("state"), lax.axis_index("plane")
    band, half = s // 2, lax.rem(s, 2)
    twin = 1 - half

    def on_plane(ring, pair):
        return {"state": s, "plane": partner(p, ring, pair)}

    def on_band(ring, pair):
        return {"state": partner(band, ring, pair) * 2 + half, "plane": p}

    on_twin = {"state": band * 2 + twin, "plane": p}

    barrier = pltpu.get_barrier_semaphore()
    for to in [on_twin] + [on_plane(*step) for step in STEPS] + [on_band(*step) for step in STEPS]:
        pl.semaphore_signal(barrier, inc=1, device_id=to, device_id_type=MESH)

    loads = {}
    for at, name in enumerate(LOADED):
        loads[name] = pltpu.make_async_copy(away[at], near_by[at], load_sem.at[at])
    for name in FIRST:
        loads[name].start()

    def loaded(*names):
        for name in names:
            loads[name].wait()
        return [near_by[LOADED.index(name)] for name in names]

    count = [0]

    def post(src, dst, to):
        at = count[0]
        count[0] += 1
        copy = pltpu.make_async_remote_copy(
            src_ref=src, dst_ref=dst, send_sem=send.at[at], recv_sem=recv.at[at], device_id=to, device_id_type=MESH
        )
        copy.start()
        return copy

    def done(copies):
        for copy in copies:
            copy.wait()

    def rows_of(other):
        return pl.ds(pl.multiple_of(other * 8, 8), 8)

    def lanes_of(part):
        return pl.ds(pl.multiple_of(part * 1024, 1024), 1024)

    coeffs, mask, zin = loaded("coeffs", "mask", "zin")
    for name in LOADED[len(FIRST) :]:
        loads[name].start()
    fetch = pltpu.make_async_copy(along.at[band], kernel_z, kernel_sem)
    fetch.start()
    values = (coeffs[...] * mask[...].astype(F32)[None]).reshape(2 * NZ, CHUNK)
    held[...] = table_first(zin, values).reshape(PLANES, 32, CHUNK)
    pl.semaphore_wait(barrier, 15)
    copies = [post(held.at[partner(p, *step)], sticks.at[p], on_plane(*step)) for step in STEPS]
    sticks[p] = held[p]

    cols, = loaded("cols")

    def place(chunk, fresh):
        col = columns_of(cols, chunk)
        above = one_hot(col >> 8, 32).astype(BF16)[None]
        below = one_hot(col & 255, 256).astype(BF16)
        high, low = parts(sticks[chunk])
        below = jnp.concatenate([below, below], axis=1)
        for first in (0, 16):
            left = jnp.concatenate(
                [(part[first : first + 16, None, :] * above).reshape(512, CHUNK) for part in (high, low)], axis=1
            )
            rows = slice(first * 32, first * 32 + 512)
            if fresh:
                grid[rows] = dot_t(left, below)
            else:
                grid[rows] += dot_t(left, below)

    place(p, True)
    for copy, (ring, pair) in reversed(list(zip(copies, STEPS))):
        copy.wait()
        place(partner(p, 4 - ring, pair), False)

    yin, xin, core, xmid = loaded("yin", "xin", "core", "xmid")
    def waves(part):
        lines = []
        for odd in range(2):
            rows = [
                grid[pl.ds(pl.multiple_of(c * 512 + part * 256, 256), 256), odd * 128 : odd * 128 + 128] for c in range(2)
            ]
            turned = table_last(jnp.concatenate(rows, axis=1), yin)
            lines.append(
                [
                    jnp.concatenate(
                        [turned[z * 32 : z * 32 + 32, c * 128 : c * 128 + 128] for z in range(8)], axis=1
                    )
                    for c in range(2)
                ]
            )
        lines = jnp.concatenate([lines[odd][c] for c in range(2) for odd in range(2)], axis=0)
        wave = four_first(xin, lines)
        psi[:, lanes_of(part)] = wave
        return (wave[:64] * wave[:64] + wave[64:] * wave[64:]) * (1.0 / STATES)

    to_twin[...] = waves(twin)
    copy = post(to_twin, from_twin, on_twin)
    own = waves(half)
    copy.wait()
    summed[...] = own + from_twin[...]

    copies = [post(summed.at[rows_of(partner(band, *step)), :], given.at[band], on_band(*step)) for step in STEPS]
    rho = jnp.concatenate([core[half * 8 + z, rows_of(band), :] for z in range(8)], axis=1)
    rho = rho + summed[rows_of(band), :]
    for copy, (ring, pair) in reversed(list(zip(copies, STEPS))):
        copy.wait()
        rho = rho + given[partner(band, 4 - ring, pair)]
    block[...] = rho

    def all_bands(src, dst):
        return [post(src, dst.at[rows_of(band), :], on_band(*step)) for step in STEPS]

    def all_planes(src, dst):
        return [post(src, dst.at[p], on_plane(*step)) for step in STEPS]

    class Along:
        def __init__(self, copies, source, weight, slot):
            self.arrivals = list(reversed(list(zip(copies, STEPS))))
            self.source, self.weight, self.slot = source, weight, slot
            self.sums = [[jnp.zeros((8, 128), F32)] * 8 for _ in range(2)]
            self.add(p)

        def add(self, other):
            held = [self.source[other, :, z * 128 : z * 128 + 128] for z in range(8)]
            for sums, part in zip(self.sums, (half, twin)):
                start = (p - other) * 16 + (part - half) * 8 + 128
                factors = {shift: self.weight(start + shift) for shift in range(-7, 8)}
                for to in range(8):
                    for z in range(8):
                        sums[to] = sums[to] + factors[to - z] * held[z]

        def take(self, number):
            for copy, (ring, pair) in self.arrivals[:number]:
                copy.wait()
                self.add(partner(p, 4 - ring, pair))
            self.arrivals = self.arrivals[number:]

        def swap(self):
            self.take(len(self.arrivals))
            partial[self.slot, 0] = jnp.concatenate(self.sums[1], axis=1)
            self.copy = post(partial.at[self.slot, 0], partial.at[self.slot, 1], on_twin)

        def result(self):
            self.copy.wait()
            return jnp.concatenate(self.sums[0], axis=1) + partial[self.slot, 1]

    def slope(at):
        return dz[at]

    def mixed_x(source):
        high, low = parts(source[...])
        return dot(xmid[0, band], high) + dot(xmid[0, band], low) + dot(xmid[1, band], high)

    dz, dy, hy, hx, xout, yout = loaded("dz", "dy", "hy", "hx", "xout", "yout")
    by_x[rows_of(band), :] = rho
    by_z[p] = rho
    z_copies, x_copies = all_planes(block, by_z), all_bands(block, by_x)
    grad_z = Along(z_copies, by_z, slope, 0)
    grad_y = untile(table_last(tiles(rho, 8), dy), 8)
    grad_z.take(3)
    done(x_copies)
    both = mixed_x(by_x)
    grad_x = both[:8]
    rho_xy = untile(table_last(tiles(both[8:], 8), hy), 8)
    rho_hat[...] = rho_xy
    r_copies = all_planes(rho_hat, by_z3)
    by_z3[p] = rho_xy
    grad_z.swap()
    fetch.wait()

    def even(at):
        at = lax.rem(at, 128)
        return kernel_z[jnp.minimum(at, 128 - at)]

    spread = Along(r_copies, by_z3, even, 1)
    grad_z = grad_z.result()

    v_local, twice = xc_terms(rho, grad_z * grad_z + grad_x * grad_x + grad_y * grad_y)
    flux = twice * grad_z
    flux_z[...] = flux
    z_copies = all_planes(flux_z, by_z2)
    by_z2[p] = flux
    flux = twice * grad_x
    flux_x[...] = flux
    x_copies = all_bands(flux_x, by_x2)
    by_x2[rows_of(band), :] = flux
    total = v_local - untile(table_last(tiles(twice * grad_y, 8), dy), 8)

    slant = Along(z_copies, by_z2, slope, 2)
    spread.swap()
    slant.take(3)
    spread = spread.result()
    far_own[...] = spread
    f_copies = all_bands(far_own, far)
    far[rows_of(band), :] = spread
    slant.swap()
    done(x_copies)
    total = total - mixed_x(by_x2)[:8]
    total = total - slant.result()
    near_own[...] = total
    n_copies = all_bands(near_own, near)
    near[rows_of(band), :] = total

    done(f_copies)
    turned = untile(table_last(tiles(four_first(hx, far[...]), 64), hy), 64)
    done(n_copies)
    pot[...] = near[...] + turned
    copy = post(pot, pot_twin, on_twin)

    def forces(potential, part):
        lanes = lanes_of(part)
        wave = psi[:, lanes]
        wave = jnp.concatenate([potential * wave[:64], potential * wave[64:]], axis=0)
        wave = four_first(xout, wave)
        for odd in range(2):
            rows = []
            for c in range(2):
                first = c * 64 + odd * 32
                rows.append(
                    jnp.concatenate([wave[first : first + 32, z * 128 : z * 128 + 128] for z in range(8)], axis=0)
                )
            turned = table_last(jnp.concatenate(rows, axis=1), yout)
            for c in range(2):
                at = pl.ds(pl.multiple_of(c * 512 + part * 256, 256), 256)
                grid[at, odd * 128 : odd * 128 + 128] = turned[:, c * 128 : c * 128 + 128]

    forces(pot[...], half)
    copy.wait()
    forces(pot_twin[...], twin)

    high, low = parts(grid[...])
    left = jnp.concatenate([high, low], axis=1)
    copies = []
    order = STEPS + ((0, 0),)
    for first in range(0, PLANES, 2):
        steps = order[first : first + 2]
        owners = [partner(p, *step) for step in steps]
        col = jnp.concatenate([columns_of(cols, owner) for owner in owners], axis=1)
        above = one_hot(col >> 8, 32)[None]
        below = one_hot(col & 255, 256).astype(BF16)
        below = jnp.concatenate([below, below], axis=0)
        found = [
            jnp.sum(dot(left[rows : rows + 512], below).reshape(16, 32, 2 * CHUNK) * above, axis=1)
            for rows in (0, 512)
        ]
        found = jnp.concatenate(found, axis=0)
        for at, (step, owner) in enumerate(zip(steps, owners)):
            chunk = found[:, at * CHUNK : (at + 1) * CHUNK]
            picked[owner] = chunk
            if step == (0, 0):
                fetch = pltpu.make_async_copy(picked.at[p], back.at[p], kernel_sem)
                fetch.start()
                copies.append(fetch)
            else:
                copies.append(post(picked.at[owner], back.at[p], on_plane(*step)))
    done(copies)


def last_kernel(back, mask, zout, out):
    force = table_first(zout, back[...].reshape(256, CHUNK)).reshape(2, NZ, CHUNK)
    out[...] = force * mask[...].astype(F32)[None]


COPIES = 7 * 10 + 5


def call(kernel, outs, ins, in_specs, out_specs, scratch=(), collective=None, limit=60):
    return pl.pallas_call(
        kernel,
        out_shape=[jax.ShapeDtypeStruct(shape, F32) for shape in outs],
        in_specs=in_specs,
        out_specs=out_specs,
        scratch_shapes=scratch,
        compiler_params=pltpu.CompilerParams(
            collective_id=collective,
            has_side_effects=collective is not None,
            vmem_limit_bytes=limit * 1024 * 1024,
        ),
    )(*ins)


def on_device(coeffs, mask, stick_cols, core):
    t = {name: jnp.asarray(table) for name, table in tables().items()}
    t.update(coeffs=coeffs.reshape(2, NZ, CHUNK), mask=mask, cols=stick_cols.reshape(1, NSTICK), core=core)
    bundle, own, all_x, all_z = (PLANES, 32, CHUNK), (8, 1024), (64, 1024), (PLANES, 8, 1024)
    shapes = [bundle, bundle, (1024, 256), (128, 2048), (3, 2, 8, 1024), all_x, all_z]
    shapes += [own] * 6 + [all_x] * 2
    shapes += [all_x] * 2 + [all_z] * 3 + [(65, 8, 128)] + [all_x] * 4 + [bundle]
    anywhere, whole = pl.BlockSpec(memory_space=pl.ANY), pl.BlockSpec(memory_space=pltpu.VMEM)
    back, = call(
        step_kernel,
        [bundle],
        [t["along"]] + [t[name] for name in LOADED],
        [anywhere] * (len(LOADED) + 1),
        [anywhere],
        [
            (pltpu.SMEM if name == "dz" else pltpu.VMEM)(t[name].shape, t[name].dtype)
            for name in LOADED
        ]
        + [pltpu.VMEM(shape, F32) for shape in shapes]
        + [pltpu.SemaphoreType.DMA, pltpu.SemaphoreType.DMA((len(LOADED),))]
        + [pltpu.SemaphoreType.DMA((COPIES,)), pltpu.SemaphoreType.DMA((COPIES,))],
        collective=0,
    )
    forces, = call(
        last_kernel,
        [(2, NZ, CHUNK)],
        [back, mask, t["zout"]],
        [whole] * 3,
        [whole],
        limit=8,
    )
    return forces.reshape(2, 1, NZ, CHUNK)


def solution(mesh):
    in_specs = (P(None, "state", None, "plane"), P(None, "plane"), P(), P("plane", None, None))
    out_specs = P(None, "state", None, "plane")
    return jax.shard_map(
        on_device, mesh=mesh, in_specs=in_specs, out_specs=out_specs, check_vma=False
    )
```

```python
import functools
import math

import jax
import jax.numpy as jnp
import ml_dtypes
import numpy as np
from jax import lax
from jax.experimental import pallas as pl
from jax.experimental.pallas import tpu as pltpu
from jax.sharding import PartitionSpec as P

NZ = 128
NX = 64
NY = 128
NSTICK = 3072
STATES = 16
PLANES = 8
CHUNK = NSTICK // PLANES
SPACING = 0.5
CELLS = NX * NY * NZ
NORM = 1.0 / math.sqrt(4.0 * NSTICK * NZ)
F32 = jnp.float32
BF16 = jnp.bfloat16
MESH = pl.DeviceIdType.MESH


def two_parts(table):
    high = np.asarray(table, np.float64).astype(ml_dtypes.bfloat16)
    low = (np.asarray(table, np.float64) - high.astype(np.float64)).astype(ml_dtypes.bfloat16)
    return np.stack([high, low])


def wave_table(out_freq, in_freq, count, sign):
    angle = 2.0 * np.pi * (np.outer(out_freq, in_freq) % count) / count
    cos, sin = np.cos(angle), sign * np.sin(angle)
    return np.block([[cos, -sin], [sin, cos]])


def derivative_matrix(count):
    signed = np.arange(count)
    signed = np.where(signed >= count // 2, signed - count, signed)
    deriv = np.where(signed == -(count // 2), 0, signed) * 2.0 * np.pi / (count * SPACING)
    return np.real(np.fft.ifft(1j * deriv[:, None] * np.fft.fft(np.eye(count), axis=0), axis=0))


def cas_matrix(count):
    angle = 2.0 * np.pi * (np.outer(np.arange(count), np.arange(count)) % count) / count
    return np.cos(angle) + np.sin(angle)


def squared_freq(count):
    signed = np.arange(count)
    signed = np.where(signed >= count // 2, signed - count, signed)
    return (signed * 2.0 * np.pi / (count * SPACING)) ** 2


def four_parts(table):
    high, low = two_parts(table)
    return np.block([[high, high], [low, low]])


@functools.cache
def tables():
    steps = np.arange(128)
    zwave = wave_table(steps, steps, NZ, 1.0).reshape(2, PLANES, 16, 256)
    zin = NORM * zwave.transpose(1, 0, 2, 3).reshape(256, 256)
    zwave = wave_table(steps, steps, NZ, -1.0).reshape(256, 2, PLANES, 16)
    zout = -zwave.transpose(0, 2, 1, 3).reshape(256, 256) / (CELLS * NORM)
    yin = wave_table(steps, steps, NY, 1.0).T
    yout = wave_table(steps, steps, NY, -1.0).T
    gx = np.concatenate([np.arange(0, NX, 2), np.arange(1, NX, 2)])
    xin = wave_table(np.arange(NX), gx, NX, 1.0)
    xout = wave_table(gx, np.arange(NX), NX, -1.0)
    dx, hx = derivative_matrix(NX), cas_matrix(NX)
    bands = np.stack([dx.reshape(8, 8, 8, 8), hx.reshape(8, 8, 8, 8)], axis=1)
    xmid = []
    for band in range(8):
        ring = bands[[band, band ^ 1]][:, :, :, band % 2 :: 2]
        xmid.append(ring.reshape(32, 32))
    xmid = np.stack(xmid)
    dz = derivative_matrix(NZ)[:, 0]
    dz = np.concatenate([dz, dz, dz]).astype(np.float32)
    g_sq = squared_freq(NZ)[:, None, None] + squared_freq(NX)[None, :, None] + squared_freq(NY)[None, None, :]
    hart = np.where(g_sq > 0, 4.0 * np.pi / np.where(g_sq > 0, g_sq, 1.0), 0.0)
    along = np.real(np.fft.ifft(hart, axis=0))[: NZ // 2 + 1] / (NX * NY)
    along = along.reshape(65, 8, 8, NY).transpose(1, 0, 2, 3).astype(np.float32)
    return {
        "zin": two_parts(zin),
        "zout": two_parts(zout),
        "yin": two_parts(yin),
        "yout": two_parts(yout),
        "xin": four_parts(xin),
        "xout": four_parts(xout),
        "xmid": two_parts(xmid),
        "dy": two_parts(derivative_matrix(NY).T),
        "hy": two_parts(cas_matrix(NY)),
        "hx": four_parts(hx),
        "dz": dz,
        "along": along,
    }


def parts(values):
    high = values.astype(BF16)
    return high, (values - high.astype(F32)).astype(BF16)


def dot(a, b):
    return jnp.dot(a, b, preferred_element_type=F32)


def dot_t(a, b):
    return lax.dot_general(a, b, (((1,), (1,)), ((), ())), preferred_element_type=F32)


def table_first(table, values):
    high, low = parts(values)
    return dot(table[0], high) + dot(table[0], low) + dot(table[1], high)


def four_first(table, values):
    both = dot(table[...], jnp.concatenate(parts(values), axis=0))
    half = table.shape[0] // 2
    return both[:half] + both[half:]


def table_last(values, table):
    high, low = parts(values)
    return dot(high, table[0]) + dot(low, table[0]) + dot(high, table[1])


def one_hot(values, rows):
    places = lax.broadcasted_iota(jnp.int32, (rows, values.shape[1]), 0)
    return jnp.where(places == values, 1.0, 0.0)


def columns_of(cols, chunk):
    return cols[:, pl.ds(pl.multiple_of(chunk * CHUNK, 128), CHUNK)]


def xc_terms(rho, g):
    kappa, mu = 0.804, 0.2195
    exch = 0.75 * (3.0 / math.pi) ** (1.0 / 3.0)
    scale = 1.0 / (4.0 * (3.0 * math.pi**2) ** (2.0 / 3.0))
    root = jnp.exp(jnp.log(rho) * (1.0 / 3.0))
    root = root - (root * root * root - rho) / (3.0 * root * root)
    four = rho * root
    s2 = scale * g / (four * four)
    q = 1.0 / (1.0 + s2 * (mu / kappa))
    enhance = 1.0 + kappa - kappa * q
    radius = (3.0 / (4.0 * math.pi)) ** (1.0 / 3.0) / root
    inverse = 1.0 / (7.8 + radius)
    v_local = -exch * root * ((4.0 / 3.0) * enhance - (8.0 / 3.0) * mu * s2 * q * q)
    v_local = v_local - 0.44 * inverse - (0.44 / 3.0) * radius * inverse * inverse
    return v_local, (-2.0 * exch * mu * scale) * q * q / four


def tiles(block, count):
    return jnp.concatenate([block[:, z * 128 : z * 128 + 128] for z in range(8)], axis=0)


def untile(rows, count):
    return jnp.concatenate([rows[z * count : z * count + count] for z in range(8)], axis=1)


STEPS = ((2, 1), (1, 1), (3, 1), (0, 1), (2, 0), (1, 0), (3, 0))


def partner(place, ring, pair):
    return lax.rem(place // 2 + ring, 4) * 2 + lax.rem(place + pair, 2)


FIRST = ("coeffs", "mask", "zin")
LOADED = FIRST + ("cols", "dz", "yin", "xin", "core", "xmid", "dy", "hy", "hx", "xout", "yout")


def step_kernel(along, *refs):
    away, (back, *refs) = refs[: len(LOADED)], refs[len(LOADED) :]
    work(along, away, back, refs[: len(LOADED)], *refs[len(LOADED) :])


def work(
    along, away, back, near_by,
    held, sticks, grid, psi, partial, summed, given,
    block, flux_x, flux_z, rho_hat, near_own, far_own, to_twin, from_twin,
    crossed, by_x, by_x2, by_z, by_z2, by_z3, kernel_z, near, far, pot, pot_twin, picked,
    kernel_sem, load_sem, send, recv,
):
    s, p = lax.axis_index("state"), lax.axis_index("plane")
    band, half = s // 2, lax.rem(s, 2)
    twin = 1 - half

    def on_plane(ring, pair):
        return {"state": s, "plane": partner(p, ring, pair)}

    def on_band(ring, pair):
        return {"state": partner(band, ring, pair) * 2 + half, "plane": p}

    on_twin = {"state": band * 2 + twin, "plane": p}

    barrier = pltpu.get_barrier_semaphore()
    for to in [on_twin] + [on_plane(*step) for step in STEPS] + [on_band(*step) for step in STEPS]:
        pl.semaphore_signal(barrier, inc=1, device_id=to, device_id_type=MESH)

    loads = {}
    for at, name in enumerate(LOADED):
        loads[name] = pltpu.make_async_copy(away[at], near_by[at], load_sem.at[at])
    for name in FIRST:
        loads[name].start()

    def loaded(*names):
        for name in names:
            loads[name].wait()
        return [near_by[LOADED.index(name)] for name in names]

    count = [0]

    def post(src, dst, to):
        at = count[0]
        count[0] += 1
        copy = pltpu.make_async_remote_copy(
            src_ref=src, dst_ref=dst, send_sem=send.at[at], recv_sem=recv.at[at], device_id=to, device_id_type=MESH
        )
        copy.start()
        return copy

    def done(copies):
        for copy in copies:
            copy.wait()

    def rows_of(other):
        return pl.ds(pl.multiple_of(other * 8, 8), 8)

    def lanes_of(part):
        return pl.ds(pl.multiple_of(part * 1024, 1024), 1024)

    coeffs, mask, zin = loaded("coeffs", "mask", "zin")
    for name in LOADED[len(FIRST) :]:
        loads[name].start()
    fetch = pltpu.make_async_copy(along.at[band], kernel_z, kernel_sem)
    fetch.start()
    values = (coeffs[...] * mask[...].astype(F32)[None]).reshape(2 * NZ, CHUNK)
    held[...] = table_first(zin, values).reshape(PLANES, 32, CHUNK)
    pl.semaphore_wait(barrier, 15)
    copies = [post(held.at[partner(p, *step)], sticks.at[p], on_plane(*step)) for step in STEPS]
    sticks[p] = held[p]

    cols, = loaded("cols")

    def place(chunk, fresh):
        col = columns_of(cols, chunk)
        above = one_hot(col >> 8, 32).astype(BF16)[None]
        below = one_hot(col & 255, 256).astype(BF16)
        high, low = parts(sticks[chunk])
        below = jnp.concatenate([below, below], axis=1)
        for first in (0, 16):
            left = jnp.concatenate(
                [(part[first : first + 16, None, :] * above).reshape(512, CHUNK) for part in (high, low)], axis=1
            )
            rows = slice(first * 32, first * 32 + 512)
            if fresh:
                grid[rows] = dot_t(left, below)
            else:
                grid[rows] += dot_t(left, below)

    place(p, True)
    for copy, (ring, pair) in reversed(list(zip(copies, STEPS))):
        copy.wait()
        place(partner(p, 4 - ring, pair), False)

    yin, xin, core, xmid = loaded("yin", "xin", "core", "xmid")
    def waves(part, quarter):
        lines = []
        for odd in range(2):
            rows = [
                grid[
                    pl.ds(pl.multiple_of(c * 512 + part * 256 + quarter * 128, 128), 128),
                    odd * 128 : odd * 128 + 128,
                ]
                for c in range(2)
            ]
            turned = table_last(jnp.concatenate(rows, axis=1), yin)
            lines.append(
                [
                    jnp.concatenate(
                        [turned[z * 32 : z * 32 + 32, c * 128 : c * 128 + 128] for z in range(4)], axis=1
                    )
                    for c in range(2)
                ]
            )
        lines = jnp.concatenate([lines[odd][c] for c in range(2) for odd in range(2)], axis=0)
        wave = four_first(xin, lines)
        psi[:, pl.ds(pl.multiple_of(part * 1024 + quarter * 512, 512), 512)] = wave
        return (wave[:64] * wave[:64] + wave[64:] * wave[64:]) * (1.0 / STATES)

    cuts = [slice(0, 512), slice(512, 1024)]
    swaps = []
    for quarter, cut in enumerate(cuts):
        to_twin[:, cut] = waves(twin, quarter)
        swaps.append(post(to_twin.at[:, cut], from_twin.at[:, cut], on_twin))

    copies = []
    for quarter, cut in enumerate(cuts):
        own = waves(half, quarter)
        swaps[quarter].wait()
        summed[:, cut] = own + from_twin[:, cut]
        copies.append(
            [
                post(summed.at[rows_of(partner(band, *step)), cut], given.at[band, :, cut], on_band(*step))
                for step in STEPS
            ]
        )
    rho = jnp.concatenate([core[half * 8 + z, rows_of(band), :] for z in range(8)], axis=1)
    rho = rho + summed[rows_of(band), :]
    for first, second, (ring, pair) in reversed(list(zip(*copies, STEPS))):
        first.wait()
        second.wait()
        rho = rho + given[partner(band, 4 - ring, pair)]
    block[...] = rho

    def all_bands(src, dst):
        return [post(src, dst.at[rows_of(band), :], on_band(*step)) for step in STEPS]

    def all_planes(src, dst):
        return [post(src, dst.at[p], on_plane(*step)) for step in STEPS]

    class Along:
        def __init__(self, copies, source, weight, slot):
            self.arrivals = list(reversed(list(zip(copies, STEPS))))
            self.source, self.weight, self.slot = source, weight, slot
            self.sums = [[jnp.zeros((8, 128), F32)] * 8 for _ in range(2)]
            self.add(p)

        def add(self, other):
            held = [self.source[other, :, z * 128 : z * 128 + 128] for z in range(8)]
            for sums, part in zip(self.sums, (half, twin)):
                start = (p - other) * 16 + (part - half) * 8 + 128
                factors = {shift: self.weight(start + shift) for shift in range(-7, 8)}
                for to in range(8):
                    for z in range(8):
                        sums[to] = sums[to] + factors[to - z] * held[z]

        def take(self, number):
            for copy, (ring, pair) in self.arrivals[:number]:
                copy.wait()
                self.add(partner(p, 4 - ring, pair))
            self.arrivals = self.arrivals[number:]

        def swap(self):
            self.take(len(self.arrivals))
            partial[self.slot, 0] = jnp.concatenate(self.sums[1], axis=1)
            self.copy = post(partial.at[self.slot, 0], partial.at[self.slot, 1], on_twin)

        def result(self):
            self.copy.wait()
            return jnp.concatenate(self.sums[0], axis=1) + partial[self.slot, 1]

    def slope(at):
        return dz[at]

    def all_ring(src, dst):
        return [post(src, dst.at[rows_of(band // 2), :], on_band(*step)) for step in STEPS if step[1] == 0]

    def mix_x(source, slot, count):
        high, low = parts(source[...])
        both = dot(xmid[0, band], high) + dot(xmid[0, band], low) + dot(xmid[1, band], high)
        crossed[slot, 0, :count] = both[16 : 16 + count]
        copy = post(crossed.at[slot, 0, :count], crossed.at[slot, 1, :count], on_band(0, 1))

        def result():
            copy.wait()
            return both[:count] + crossed[slot, 1, :count]

        return result

    dz, dy, hy, hx, xout, yout = loaded("dz", "dy", "hy", "hx", "xout", "yout")
    by_x[rows_of(band // 2), :] = rho
    by_z[p] = rho
    x_copies, z_copies = all_ring(block, by_x), all_planes(block, by_z)
    grad_z = Along(z_copies, by_z, slope, 0)
    grad_y = untile(table_last(tiles(rho, 8), dy), 8)
    done(x_copies)
    both = mix_x(by_x, 0, 16)
    grad_z.take(3)
    both = both()
    grad_x = both[:8]
    rho_xy = untile(table_last(tiles(both[8:], 8), hy), 8)
    rho_hat[...] = rho_xy
    r_copies = all_planes(rho_hat, by_z3)
    by_z3[p] = rho_xy
    grad_z.swap()
    fetch.wait()

    def even(at):
        at = lax.rem(at, 128)
        return kernel_z[jnp.minimum(at, 128 - at)]

    spread = Along(r_copies, by_z3, even, 1)
    grad_z = grad_z.result()

    v_local, twice = xc_terms(rho, grad_z * grad_z + grad_x * grad_x + grad_y * grad_y)
    flux = twice * grad_x
    flux_x[...] = flux
    x_copies = all_ring(flux_x, by_x2)
    by_x2[rows_of(band // 2), :] = flux
    flux = twice * grad_z
    flux_z[...] = flux
    z_copies = all_planes(flux_z, by_z2)
    by_z2[p] = flux
    total = v_local - untile(table_last(tiles(twice * grad_y, 8), dy), 8)

    slant = Along(z_copies, by_z2, slope, 2)
    spread.swap()
    done(x_copies)
    slope_x = mix_x(by_x2, 1, 8)
    spread = spread.result()
    far_own[...] = spread
    f_copies = all_bands(far_own, far)
    far[rows_of(band), :] = spread
    slant.swap()
    total = total - slope_x()
    total = total - slant.result()
    near_own[...] = total
    n_copies = all_bands(near_own, near)
    near[rows_of(band), :] = total

    done(f_copies)
    turned = untile(table_last(tiles(four_first(hx, far[...]), 64), hy), 64)
    done(n_copies)
    pot[...] = near[...] + turned
    copy = post(pot, pot_twin, on_twin)

    def forces(potential, part):
        lanes = lanes_of(part)
        wave = psi[:, lanes]
        wave = jnp.concatenate([potential * wave[:64], potential * wave[64:]], axis=0)
        wave = four_first(xout, wave)
        for odd in range(2):
            rows = []
            for c in range(2):
                first = c * 64 + odd * 32
                rows.append(
                    jnp.concatenate([wave[first : first + 32, z * 128 : z * 128 + 128] for z in range(8)], axis=0)
                )
            turned = table_last(jnp.concatenate(rows, axis=1), yout)
            for c in range(2):
                at = pl.ds(pl.multiple_of(c * 512 + part * 256, 256), 256)
                grid[at, odd * 128 : odd * 128 + 128] = turned[:, c * 128 : c * 128 + 128]

    order = STEPS + ((0, 0),)

    def places_of(steps):
        owners = [partner(p, *step) for step in steps]
        col = jnp.concatenate([columns_of(cols, owner) for owner in owners], axis=1)
        above = one_hot(col >> 8, 32)[None]
        below = one_hot(col & 255, 256).astype(BF16)
        return owners, above, jnp.concatenate([below, below], axis=0)

    def pick(at, above, below):
        rows = grid[at, :]
        found = dot(jnp.concatenate(parts(rows), axis=1), below)
        return jnp.sum(found.reshape(-1, 32, 2 * CHUNK) * above, axis=1)

    def pick_half(owners, above, below, part):
        for c in range(2):
            found = pick(pl.ds(pl.multiple_of(c * 512 + part * 256, 256), 256), above, below)
            for at, owner in enumerate(owners):
                picked[owner, pl.ds(pl.multiple_of(c * 16 + part * 8, 8), 8), :] = found[
                    :, at * CHUNK : (at + 1) * CHUNK
                ]

    forces(pot[...], half)
    ahead = places_of(order[:2])
    pick_half(*ahead, half)
    copy.wait()
    forces(pot_twin[...], twin)
    pick_half(*ahead, twin)
    copies = [
        post(picked.at[owner], back.at[p], on_plane(*step)) for step, owner in zip(order[:2], ahead[0])
    ]
    for first in range(2, PLANES, 2):
        steps = order[first : first + 2]
        owners, above, below = places_of(steps)
        for c in range(2):
            found = pick(slice(c * 512, c * 512 + 512), above, below)
            for at, owner in enumerate(owners):
                picked[owner, c * 16 : c * 16 + 16, :] = found[:, at * CHUNK : (at + 1) * CHUNK]
        for step, owner in zip(steps, owners):
            if step == (0, 0):
                fetch = pltpu.make_async_copy(picked.at[p], back.at[p], kernel_sem)
                fetch.start()
                copies.append(fetch)
            else:
                copies.append(post(picked.at[owner], back.at[p], on_plane(*step)))
    done(copies)


def last_kernel(back, mask, zout, out):
    force = table_first(zout, back[...].reshape(256, CHUNK)).reshape(2, NZ, CHUNK)
    out[...] = force * mask[...].astype(F32)[None]


COPIES = 7 * 9 + 2 * 3 + 4 + 4


def call(kernel, outs, ins, in_specs, out_specs, scratch=(), collective=None, limit=60):
    return pl.pallas_call(
        kernel,
        out_shape=[jax.ShapeDtypeStruct(shape, F32) for shape in outs],
        in_specs=in_specs,
        out_specs=out_specs,
        scratch_shapes=scratch,
        compiler_params=pltpu.CompilerParams(
            collective_id=collective,
            has_side_effects=collective is not None,
            vmem_limit_bytes=limit * 1024 * 1024,
        ),
    )(*ins)


def on_device(coeffs, mask, stick_cols, core):
    t = {name: jnp.asarray(table) for name, table in tables().items()}
    t.update(coeffs=coeffs.reshape(2, NZ, CHUNK), mask=mask, cols=stick_cols.reshape(1, NSTICK), core=core)
    bundle, own, all_x, all_z = (PLANES, 32, CHUNK), (8, 1024), (64, 1024), (PLANES, 8, 1024)
    shapes = [bundle, bundle, (1024, 256), (128, 2048), (3, 2, 8, 1024), all_x, all_z]
    shapes += [own] * 6 + [all_x] * 2
    shapes += [(2, 2, 16, 1024)] + [(32, 1024)] * 2 + [all_z] * 3 + [(65, 8, 128)] + [all_x] * 4 + [bundle]
    anywhere, whole = pl.BlockSpec(memory_space=pl.ANY), pl.BlockSpec(memory_space=pltpu.VMEM)
    back, = call(
        step_kernel,
        [bundle],
        [t["along"]] + [t[name] for name in LOADED],
        [anywhere] * (len(LOADED) + 1),
        [anywhere],
        [
            (pltpu.SMEM if name == "dz" else pltpu.VMEM)(t[name].shape, t[name].dtype)
            for name in LOADED
        ]
        + [pltpu.VMEM(shape, F32) for shape in shapes]
        + [pltpu.SemaphoreType.DMA, pltpu.SemaphoreType.DMA((len(LOADED),))]
        + [pltpu.SemaphoreType.DMA((COPIES,)), pltpu.SemaphoreType.DMA((COPIES,))],
        collective=0,
    )
    forces, = call(
        last_kernel,
        [(2, NZ, CHUNK)],
        [back, mask, t["zout"]],
        [whole] * 3,
        [whole],
        limit=8,
    )
    return forces.reshape(2, 1, NZ, CHUNK)


def solution(mesh):
    in_specs = (P(None, "state", None, "plane"), P(None, "plane"), P(), P("plane", None, None))
    out_specs = P(None, "state", None, "plane")
    return jax.shard_map(
        on_device, mesh=mesh, in_specs=in_specs, out_specs=out_specs, check_vma=False
    )
```

```python
import functools
import math

import jax
import jax.numpy as jnp
import ml_dtypes
import numpy as np
from jax import lax
from jax.experimental import pallas as pl
from jax.experimental.pallas import tpu as pltpu
from jax.sharding import PartitionSpec as P

NZ = 128
NX = 64
NY = 128
NSTICK = 3072
STATES = 16
PLANES = 8
CHUNK = NSTICK // PLANES
SPACING = 0.5
CELLS = NX * NY * NZ
NORM = 1.0 / math.sqrt(4.0 * NSTICK * NZ)
F32 = jnp.float32
BF16 = jnp.bfloat16
MESH = pl.DeviceIdType.MESH


STEPS = ((2, 1), (1, 1), (3, 1), (0, 1), (2, 0), (1, 0), (3, 0))


def two_parts(table):
    high = np.asarray(table, np.float64).astype(ml_dtypes.bfloat16)
    low = (np.asarray(table, np.float64) - high.astype(np.float64)).astype(ml_dtypes.bfloat16)
    return np.stack([high, low])


def wave_table(out_freq, in_freq, count, sign):
    angle = 2.0 * np.pi * (np.outer(out_freq, in_freq) % count) / count
    cos, sin = np.cos(angle), sign * np.sin(angle)
    return np.block([[cos, -sin], [sin, cos]])


def derivative_matrix(count):
    signed = np.arange(count)
    signed = np.where(signed >= count // 2, signed - count, signed)
    deriv = np.where(signed == -(count // 2), 0, signed) * 2.0 * np.pi / (count * SPACING)
    return np.real(np.fft.ifft(1j * deriv[:, None] * np.fft.fft(np.eye(count), axis=0), axis=0))


def cas_matrix(count):
    angle = 2.0 * np.pi * (np.outer(np.arange(count), np.arange(count)) % count) / count
    return np.cos(angle) + np.sin(angle)


def squared_freq(count):
    signed = np.arange(count)
    signed = np.where(signed >= count // 2, signed - count, signed)
    return (signed * 2.0 * np.pi / (count * SPACING)) ** 2


def four_parts(table):
    high, low = two_parts(table)
    return np.block([[high, high], [low, low]])


@functools.cache
def tables():
    steps = np.arange(128)
    zwave = wave_table(steps, steps, NZ, 1.0).reshape(2, PLANES, 16, 256)
    zin = NORM * zwave.transpose(1, 0, 2, 3).reshape(256, 256)
    zwave = wave_table(steps, steps, NZ, -1.0).reshape(256, 2, PLANES, 16)
    zout = -zwave.transpose(0, 2, 1, 3).reshape(256, 256) / (CELLS * NORM)
    yin = wave_table(steps, steps, NY, 1.0).T
    yout = wave_table(steps, steps, NY, -1.0).T
    gx = np.concatenate([np.arange(0, NX, 2), np.arange(1, NX, 2)])
    xin = wave_table(np.arange(NX), gx, NX, 1.0)
    xout = wave_table(gx, np.arange(NX), NX, -1.0)
    dx, hx = derivative_matrix(NX), cas_matrix(NX)
    bands = np.stack([dx.reshape(8, 8, 8, 8), hx.reshape(8, 8, 8, 8)], axis=1)
    xmid = []
    for band in range(8):
        ring = [(band // 2 - step) % 4 * 2 + band % 2 for step in [0] + [ring for ring, pair in STEPS if pair == 0]]
        ring = bands[[band, band ^ 1]][:, :, :, ring]
        xmid.append(ring.reshape(32, 32))
    xmid = np.stack(xmid)
    dz = derivative_matrix(NZ)[:, 0]
    dz = np.concatenate([dz, dz, dz]).astype(np.float32)
    g_sq = squared_freq(NZ)[:, None, None] + squared_freq(NX)[None, :, None] + squared_freq(NY)[None, None, :]
    hart = np.where(g_sq > 0, 4.0 * np.pi / np.where(g_sq > 0, g_sq, 1.0), 0.0)
    along = np.real(np.fft.ifft(hart, axis=0))[: NZ // 2 + 1] / (NX * NY)
    along = along.reshape(65, 8, 8, NY).transpose(1, 0, 2, 3).astype(np.float32)
    return {
        "zin": two_parts(zin),
        "zout": two_parts(zout),
        "yin": two_parts(yin),
        "yout": two_parts(yout),
        "xin": four_parts(xin),
        "xout": four_parts(xout),
        "xmid": two_parts(xmid),
        "dy": two_parts(derivative_matrix(NY).T),
        "hy": two_parts(cas_matrix(NY)),
        "hx": four_parts(hx),
        "dz": dz,
        "along": along,
    }


def parts(values):
    high = values.astype(BF16)
    return high, (values - high.astype(F32)).astype(BF16)


def dot(a, b):
    return jnp.dot(a, b, preferred_element_type=F32)


def dot_t(a, b):
    return lax.dot_general(a, b, (((1,), (1,)), ((), ())), preferred_element_type=F32)


def table_first(table, values):
    high, low = parts(values)
    return dot(table[0], high) + dot(table[0], low) + dot(table[1], high)


def four_first(table, values):
    both = dot(table[...], jnp.concatenate(parts(values), axis=0))
    half = table.shape[0] // 2
    return both[:half] + both[half:]


def table_last(values, table):
    high, low = parts(values)
    return dot(high, table[0]) + dot(low, table[0]) + dot(high, table[1])


def one_hot(values, rows):
    places = lax.broadcasted_iota(jnp.int32, (rows, values.shape[1]), 0)
    return jnp.where(places == values, 1.0, 0.0)


def columns_of(cols, chunk):
    return cols[:, pl.ds(pl.multiple_of(chunk * CHUNK, 128), CHUNK)]


def xc_terms(rho, g):
    kappa, mu = 0.804, 0.2195
    exch = 0.75 * (3.0 / math.pi) ** (1.0 / 3.0)
    scale = 1.0 / (4.0 * (3.0 * math.pi**2) ** (2.0 / 3.0))
    root = jnp.exp(jnp.log(rho) * (1.0 / 3.0))
    root = root - (root * root * root - rho) / (3.0 * root * root)
    four = rho * root
    s2 = scale * g / (four * four)
    q = 1.0 / (1.0 + s2 * (mu / kappa))
    enhance = 1.0 + kappa - kappa * q
    radius = (3.0 / (4.0 * math.pi)) ** (1.0 / 3.0) / root
    inverse = 1.0 / (7.8 + radius)
    v_local = -exch * root * ((4.0 / 3.0) * enhance - (8.0 / 3.0) * mu * s2 * q * q)
    v_local = v_local - 0.44 * inverse - (0.44 / 3.0) * radius * inverse * inverse
    return v_local, (-2.0 * exch * mu * scale) * q * q / four


def tiles(block, count):
    return jnp.concatenate([block[:, z * 128 : z * 128 + 128] for z in range(8)], axis=0)


def untile(rows, count):
    return jnp.concatenate([rows[z * count : z * count + count] for z in range(8)], axis=1)


def partner(place, ring, pair):
    return lax.rem(place // 2 + ring, 4) * 2 + lax.rem(place + pair, 2)


FIRST = ("coeffs", "mask", "zin")
LOADED = FIRST + ("cols", "dz", "yin", "xin", "core", "xmid", "dy", "hy", "hx", "xout", "yout")


def step_kernel(along, *refs):
    away, (back, *refs) = refs[: len(LOADED)], refs[len(LOADED) :]
    work(along, away, back, refs[: len(LOADED)], *refs[len(LOADED) :])


def work(
    along, away, back, near_by,
    held, sticks, grid, psi, partial, summed, given,
    block, flux_x, flux_z, rho_hat, near_own, far_own, to_twin, from_twin,
    crossed, by_x, by_x2, by_z, by_z2, by_z3, kernel_z, near, far, pot, pot_twin, picked,
    kernel_sem, load_sem, send, recv,
):
    s, p = lax.axis_index("state"), lax.axis_index("plane")
    band, half = s // 2, lax.rem(s, 2)
    twin = 1 - half

    def on_plane(ring, pair):
        return {"state": s, "plane": partner(p, ring, pair)}

    def on_band(ring, pair):
        return {"state": partner(band, ring, pair) * 2 + half, "plane": p}

    on_twin = {"state": band * 2 + twin, "plane": p}

    barrier = pltpu.get_barrier_semaphore()
    for to in [on_twin] + [on_plane(*step) for step in STEPS] + [on_band(*step) for step in STEPS]:
        pl.semaphore_signal(barrier, inc=1, device_id=to, device_id_type=MESH)

    loads = {}
    for at, name in enumerate(LOADED):
        if name in FIRST:
            size = away[at].shape[0] // 2
            cuts = [pl.ds(side * size, size) for side in range(2)]
            loads[name] = [
                pltpu.make_async_copy(away[at].at[cut], near_by[at].at[cut], load_sem.at[side, at])
                for side, cut in enumerate(cuts)
            ]
        else:
            loads[name] = [pltpu.make_async_copy(away[at], near_by[at], load_sem.at[0, at])]
    for name in FIRST:
        for copy in loads[name]:
            copy.start()

    def loaded(*names):
        for name in names:
            for copy in loads[name]:
                copy.wait()
        return [near_by[LOADED.index(name)] for name in names]

    sent, received = [], [0]

    class Exchange:
        def __init__(self, copies, span, each=False):
            self.span, self.each, self.first = span, each, received[0]
            received[0] += len(copies) if each else 1
            self.copies = []
            for at, (src, dst, to) in enumerate(copies):
                copy = pltpu.make_async_remote_copy(
                    src_ref=src,
                    dst_ref=dst,
                    send_sem=send.at[len(sent)],
                    recv_sem=recv.at[self.first + at * each],
                    device_id=to,
                    device_id_type=MESH,
                )
                copy.start()
                self.copies.append(copy)
            sent.append(span)

        def wait(self, at=None):
            if at is None:
                pltpu.make_async_copy(self.span, self.span, recv.at[self.first]).wait()
            else:
                self.copies[at].wait_recv()

    def swap(src, dst, to):
        return Exchange([(src, dst, to)], dst)

    def rows_of(other):
        return pl.ds(pl.multiple_of(other * 8, 8), 8)

    def lanes_of(part):
        return pl.ds(pl.multiple_of(part * 1024, 1024), 1024)

    coeffs, mask, zin = loaded("coeffs", "mask", "zin")
    for name in LOADED[len(FIRST) :]:
        loads[name][0].start()
    fetch = pltpu.make_async_copy(along.at[band], kernel_z, kernel_sem)
    fetch.start()
    values = (coeffs[...] * mask[...].astype(F32)[None]).reshape(2 * NZ, CHUNK)
    held[...] = table_first(zin, values).reshape(PLANES, 32, CHUNK)
    pl.semaphore_wait(barrier, 15)
    arrivals = Exchange(
        [(held.at[partner(p, *step)], sticks.at[at], on_plane(*step)) for at, step in enumerate(STEPS)], sticks, True
    )

    cols, = loaded("cols")

    def place(values, chunk, fresh):
        col = columns_of(cols, chunk)
        above = one_hot(col >> 8, 32).astype(BF16)[None]
        below = one_hot(col & 255, 256).astype(BF16)
        high, low = parts(values)
        below = jnp.concatenate([below, below], axis=1)
        for first in (0, 16):
            left = jnp.concatenate(
                [(part[first : first + 16, None, :] * above).reshape(512, CHUNK) for part in (high, low)], axis=1
            )
            rows = slice(first * 32, first * 32 + 512)
            if fresh:
                grid[rows] = dot_t(left, below)
            else:
                grid[rows] += dot_t(left, below)

    place(held[p], p, True)
    for at, (ring, pair) in reversed(list(enumerate(STEPS))):
        arrivals.wait(at)
        place(sticks[at], partner(p, 4 - ring, pair), False)

    yin, xin, core, xmid = loaded("yin", "xin", "core", "xmid")
    def waves(part, quarter):
        lines = []
        for odd in range(2):
            rows = [
                grid[
                    pl.ds(pl.multiple_of(c * 512 + part * 256 + quarter * 128, 128), 128),
                    odd * 128 : odd * 128 + 128,
                ]
                for c in range(2)
            ]
            turned = table_last(jnp.concatenate(rows, axis=1), yin)
            lines.append(
                [
                    jnp.concatenate(
                        [turned[z * 32 : z * 32 + 32, c * 128 : c * 128 + 128] for z in range(4)], axis=1
                    )
                    for c in range(2)
                ]
            )
        lines = jnp.concatenate([lines[odd][c] for c in range(2) for odd in range(2)], axis=0)
        wave = four_first(xin, lines)
        psi[:, pl.ds(pl.multiple_of(part * 1024 + quarter * 512, 512), 512)] = wave
        return (wave[:64] * wave[:64] + wave[64:] * wave[64:]) * (1.0 / STATES)

    cuts = [slice(0, 512), slice(512, 1024)]
    swaps = []
    for quarter, cut in enumerate(cuts):
        to_twin[:, cut] = waves(twin, quarter)
        swaps.append(swap(to_twin.at[:, cut], from_twin.at[:, cut], on_twin))

    sums = []
    for quarter, cut in enumerate(cuts):
        own = waves(half, quarter)
        swaps[quarter].wait()
        summed[:, cut] = own + from_twin[:, cut]
        sums.append(
            Exchange(
                [
                    (summed.at[rows_of(partner(band, *step)), cut], given.at[at, :, cut], on_band(*step))
                    for at, step in enumerate(STEPS)
                ],
                given.at[:, :, cut],
            )
        )
    rho = jnp.concatenate([core[half * 8 + z, rows_of(band), :] for z in range(8)], axis=1)
    rho = rho + summed[rows_of(band), :]
    for part in sums:
        part.wait()
    for at in range(len(STEPS)):
        rho = rho + given[at]
    block[...] = rho

    def all_bands(src, dst):
        copies = [(src, dst.at[rows_of(band), :], on_band(*step)) for step in STEPS]
        return Exchange(copies, dst.at[pl.ds(0, 56), :])

    def all_planes(src, dst):
        return Exchange([(src, dst.at[at], on_plane(*step)) for at, step in enumerate(STEPS)], dst, True)

    class Along:
        def __init__(self, own, arrivals, source, weight, slot):
            self.arrivals, self.source, self.weight, self.slot = arrivals, source, weight, slot
            self.left = list(reversed(range(len(STEPS))))
            self.sums = [[jnp.zeros((8, 128), F32)] * 8 for _ in range(2)]
            self.add(own, p)

        def add(self, planes, other):
            held = [planes[:, z * 128 : z * 128 + 128] for z in range(8)]
            for sums, part in zip(self.sums, (half, twin)):
                start = (p - other) * 16 + (part - half) * 8 + 128
                factors = {shift: self.weight(start + shift) for shift in range(-7, 8)}
                for to in range(8):
                    for z in range(8):
                        sums[to] = sums[to] + factors[to - z] * held[z]

        def take(self, number):
            for at in self.left[:number]:
                ring, pair = STEPS[at]
                self.arrivals.wait(at)
                self.add(self.source[at], partner(p, 4 - ring, pair))
            self.left = self.left[number:]

        def swap(self):
            self.take(len(self.left))
            partial[self.slot, 0] = jnp.concatenate(self.sums[1], axis=1)
            self.copy = swap(partial.at[self.slot, 0], partial.at[self.slot, 1], on_twin)

        def result(self):
            self.copy.wait()
            return jnp.concatenate(self.sums[0], axis=1) + partial[self.slot, 1]

    def slope(at):
        return dz[at]

    def all_ring(src, dst):
        steps = [step for step in STEPS if step[1] == 0]
        copies = [(src, dst.at[at], on_band(*step)) for at, step in enumerate(steps)]
        return Exchange(copies, dst)

    def mix_x(own, source, slot, count):
        high, low = parts(jnp.concatenate([own] + [source[at] for at in range(3)], axis=0))
        both = dot(xmid[0, band], high) + dot(xmid[0, band], low) + dot(xmid[1, band], high)
        crossed[slot, 0, :count] = both[16 : 16 + count]
        copy = swap(crossed.at[slot, 0, :count], crossed.at[slot, 1, :count], on_band(0, 1))

        def result():
            copy.wait()
            return both[:count] + crossed[slot, 1, :count]

        return result

    dz, dy, hy, hx, xout, yout = loaded("dz", "dy", "hy", "hx", "xout", "yout")
    ring, planes = all_ring(block, by_x), all_planes(block, by_z)
    grad_z = Along(rho, planes, by_z, slope, 0)
    grad_y = untile(table_last(tiles(rho, 8), dy), 8)
    ring.wait()
    both = mix_x(rho, by_x, 0, 16)
    grad_z.take(3)
    both = both()
    grad_x = both[:8]
    rho_xy = untile(table_last(tiles(both[8:], 8), hy), 8)
    rho_hat[...] = rho_xy
    planes = all_planes(rho_hat, by_z3)
    grad_z.swap()
    fetch.wait()

    def even(at):
        at = lax.rem(at, 128)
        return kernel_z[jnp.minimum(at, 128 - at)]

    spread = Along(rho_xy, planes, by_z3, even, 1)
    grad_z = grad_z.result()

    v_local, twice = xc_terms(rho, grad_z * grad_z + grad_x * grad_x + grad_y * grad_y)
    along_x, across = twice * grad_x, twice * grad_z
    flux_x[...] = along_x
    ring = all_ring(flux_x, by_x2)
    flux_z[...] = across
    planes = all_planes(flux_z, by_z2)
    total = v_local - untile(table_last(tiles(twice * grad_y, 8), dy), 8)

    slant = Along(across, planes, by_z2, slope, 2)
    spread.swap()
    ring.wait()
    slope_x = mix_x(along_x, by_x2, 1, 8)
    spread = spread.result()
    far_own[...] = spread
    fars = all_bands(far_own, far)
    far[rows_of(band), :] = spread
    slant.swap()
    total = total - slope_x()
    total = total - slant.result()
    near_own[...] = total
    nears = all_bands(near_own, near)
    near[rows_of(band), :] = total

    fars.wait()
    turned = untile(table_last(tiles(four_first(hx, far[...]), 64), hy), 64)
    nears.wait()
    pot[...] = near[...] + turned
    copy = swap(pot, pot_twin, on_twin)

    def forces(potential, part):
        lanes = lanes_of(part)
        wave = psi[:, lanes]
        wave = jnp.concatenate([potential * wave[:64], potential * wave[64:]], axis=0)
        wave = four_first(xout, wave)
        for odd in range(2):
            rows = []
            for c in range(2):
                first = c * 64 + odd * 32
                rows.append(
                    jnp.concatenate([wave[first : first + 32, z * 128 : z * 128 + 128] for z in range(8)], axis=0)
                )
            turned = table_last(jnp.concatenate(rows, axis=1), yout)
            for c in range(2):
                at = pl.ds(pl.multiple_of(c * 512 + part * 256, 256), 256)
                grid[at, odd * 128 : odd * 128 + 128] = turned[:, c * 128 : c * 128 + 128]

    order = STEPS + ((0, 0),)

    def places_of(steps):
        owners = [partner(p, *step) for step in steps]
        col = jnp.concatenate([columns_of(cols, owner) for owner in owners], axis=1)
        above = one_hot(col >> 8, 32)[None]
        below = one_hot(col & 255, 256).astype(BF16)
        return owners, above, jnp.concatenate([below, below], axis=0)

    def pick(at, above, below):
        rows = grid[at, :]
        found = dot(jnp.concatenate(parts(rows), axis=1), below)
        return jnp.sum(found.reshape(-1, 32, 2 * CHUNK) * above, axis=1)

    def pick_half(owners, above, below, part):
        for c in range(2):
            found = pick(pl.ds(pl.multiple_of(c * 512 + part * 256, 256), 256), above, below)
            for at, owner in enumerate(owners):
                picked[owner, pl.ds(pl.multiple_of(c * 16 + part * 8, 8), 8), :] = found[
                    :, at * CHUNK : (at + 1) * CHUNK
                ]

    forces(pot[...], half)
    ahead = places_of(order[:2])
    pick_half(*ahead, half)
    copy.wait()
    forces(pot_twin[...], twin)
    pick_half(*ahead, twin)
    arrived = received[0]
    returns = []

    def give(step, owner):
        if step == (0, 0):
            copy = pltpu.make_async_copy(picked.at[p], back.at[p], kernel_sem)
        else:
            copy = pltpu.make_async_remote_copy(
                src_ref=picked.at[owner],
                dst_ref=back.at[p],
                send_sem=send.at[len(sent)],
                recv_sem=recv.at[arrived],
                device_id=on_plane(*step),
                device_id_type=MESH,
            )
        copy.start()
        returns.append(copy)

    for step, owner in zip(order[:2], ahead[0]):
        give(step, owner)
    for first in range(2, PLANES, 2):
        steps = order[first : first + 2]
        owners, above, below = places_of(steps)
        for c in range(2):
            found = pick(slice(c * 512, c * 512 + 512), above, below)
            for at, owner in enumerate(owners):
                picked[owner, c * 16 : c * 16 + 16, :] = found[:, at * CHUNK : (at + 1) * CHUNK]
        for step, owner in zip(steps, owners):
            give(step, owner)
    returns[-1].wait()
    seven = back.at[pl.ds(0, 7)]
    pltpu.make_async_copy(seven, seven, recv.at[arrived]).wait()
    for at, span in enumerate(sent + [seven]):
        pltpu.make_async_copy(span, span, send.at[at]).wait()


def last_kernel(back, mask, zout, out):
    force = table_first(zout, back[...].reshape(256, CHUNK)).reshape(2, NZ, CHUNK)
    out[...] = force * mask[...].astype(F32)[None]


SENDS, ARRIVALS = 19, 43


def call(kernel, outs, ins, in_specs, out_specs, scratch=(), collective=None, limit=60):
    return pl.pallas_call(
        kernel,
        out_shape=[jax.ShapeDtypeStruct(shape, F32) for shape in outs],
        in_specs=in_specs,
        out_specs=out_specs,
        scratch_shapes=scratch,
        compiler_params=pltpu.CompilerParams(
            collective_id=collective,
            has_side_effects=collective is not None,
            vmem_limit_bytes=limit * 1024 * 1024,
        ),
    )(*ins)


def on_device(coeffs, mask, stick_cols, core):
    t = {name: jnp.asarray(table) for name, table in tables().items()}
    t.update(coeffs=coeffs.reshape(2, NZ, CHUNK), mask=mask, cols=stick_cols.reshape(1, NSTICK), core=core)
    bundle, own, all_x, all_z = (PLANES, 32, CHUNK), (8, 1024), (64, 1024), (7, 8, 1024)
    shapes = [bundle, (7, 32, CHUNK), (1024, 256), (128, 2048), (3, 2, 8, 1024), all_x, all_z]
    shapes += [own] * 6 + [all_x] * 2
    shapes += [(2, 2, 16, 1024)] + [(3, 8, 1024)] * 2 + [all_z] * 3 + [(65, 8, 128)] + [all_x] * 4 + [bundle]
    anywhere, whole = pl.BlockSpec(memory_space=pl.ANY), pl.BlockSpec(memory_space=pltpu.VMEM)
    back, = call(
        step_kernel,
        [bundle],
        [t["along"]] + [t[name] for name in LOADED],
        [anywhere] * (len(LOADED) + 1),
        [anywhere],
        [
            (pltpu.SMEM if name == "dz" else pltpu.VMEM)(t[name].shape, t[name].dtype)
            for name in LOADED
        ]
        + [pltpu.VMEM(shape, F32) for shape in shapes]
        + [pltpu.SemaphoreType.DMA, pltpu.SemaphoreType.DMA((2, len(LOADED)))]
        + [pltpu.SemaphoreType.DMA((SENDS,)), pltpu.SemaphoreType.DMA((ARRIVALS,))],
        collective=0,
    )
    forces, = call(
        last_kernel,
        [(2, NZ, CHUNK)],
        [back, mask, t["zout"]],
        [whole] * 3,
        [whole],
        limit=8,
    )
    return forces.reshape(2, 1, NZ, CHUNK)


def solution(mesh):
    in_specs = (P(None, "state", None, "plane"), P(None, "plane"), P(), P("plane", None, None))
    out_specs = P(None, "state", None, "plane")
    return jax.shard_map(
        on_device, mesh=mesh, in_specs=in_specs, out_specs=out_specs, check_vma=False
    )
```

```python
import functools
import math

import jax
import jax.numpy as jnp
import ml_dtypes
import numpy as np
from jax import lax
from jax.experimental import pallas as pl
from jax.experimental.pallas import tpu as pltpu
from jax.sharding import PartitionSpec as P

NZ = 128
NX = 64
NY = 128
NSTICK = 3072
STATES = 16
PLANES = 8
CHUNK = NSTICK // PLANES
SPACING = 0.5
CELLS = NX * NY * NZ
NORM = 1.0 / math.sqrt(4.0 * NSTICK * NZ)
F32 = jnp.float32
BF16 = jnp.bfloat16
MESH = pl.DeviceIdType.MESH


STEPS = ((2, 1), (1, 1), (3, 1), (0, 1), (2, 0), (1, 0), (3, 0))


def two_parts(table):
    high = np.asarray(table, np.float64).astype(ml_dtypes.bfloat16)
    low = (np.asarray(table, np.float64) - high.astype(np.float64)).astype(ml_dtypes.bfloat16)
    return np.stack([high, low])


def wave_table(out_freq, in_freq, count, sign):
    angle = 2.0 * np.pi * (np.outer(out_freq, in_freq) % count) / count
    cos, sin = np.cos(angle), sign * np.sin(angle)
    return np.block([[cos, -sin], [sin, cos]])


def derivative_matrix(count):
    signed = np.arange(count)
    signed = np.where(signed >= count // 2, signed - count, signed)
    deriv = np.where(signed == -(count // 2), 0, signed) * 2.0 * np.pi / (count * SPACING)
    return np.real(np.fft.ifft(1j * deriv[:, None] * np.fft.fft(np.eye(count), axis=0), axis=0))


def cas_matrix(count):
    angle = 2.0 * np.pi * (np.outer(np.arange(count), np.arange(count)) % count) / count
    return np.cos(angle) + np.sin(angle)


def squared_freq(count):
    signed = np.arange(count)
    signed = np.where(signed >= count // 2, signed - count, signed)
    return (signed * 2.0 * np.pi / (count * SPACING)) ** 2


def four_parts(table):
    high, low = two_parts(table)
    return np.block([[high, high], [low, low]])


@functools.cache
def tables():
    steps = np.arange(128)
    zwave = wave_table(steps, steps, NZ, 1.0).reshape(2, PLANES, 16, 256)
    zin = NORM * zwave.transpose(1, 0, 2, 3).reshape(256, 256)
    zwave = wave_table(steps, steps, NZ, -1.0).reshape(256, 2, PLANES, 16)
    zout = -zwave.transpose(0, 2, 1, 3).reshape(256, 256) / (CELLS * NORM)
    yin = wave_table(steps, steps, NY, 1.0).T
    yout = wave_table(steps, steps, NY, -1.0).T
    gx = np.concatenate([np.arange(0, NX, 2), np.arange(1, NX, 2)])
    xin = wave_table(np.arange(NX), gx, NX, 1.0)
    xout = wave_table(gx, np.arange(NX), NX, -1.0)
    dx, hx = derivative_matrix(NX), cas_matrix(NX)
    bands = np.stack([dx.reshape(8, 8, 8, 8), hx.reshape(8, 8, 8, 8)], axis=1)
    xmid = []
    for band in range(8):
        ring = [(band // 2 - step) % 4 * 2 + band % 2 for step in [0] + [ring for ring, pair in STEPS if pair == 0]]
        ring = bands[[band, band ^ 1]][:, :, :, ring]
        xmid.append(ring.reshape(32, 32))
    xmid = np.stack(xmid)
    dz = derivative_matrix(NZ)[:, 0]
    dz = np.concatenate([dz, dz, dz]).astype(np.float32)
    g_sq = squared_freq(NZ)[:, None, None] + squared_freq(NX)[None, :, None] + squared_freq(NY)[None, None, :]
    hart = np.where(g_sq > 0, 4.0 * np.pi / np.where(g_sq > 0, g_sq, 1.0), 0.0)
    along = np.real(np.fft.ifft(hart, axis=0))[: NZ // 2 + 1] / (NX * NY)
    along = along.reshape(65, 8, 8, NY).transpose(1, 0, 2, 3).astype(np.float32)
    return {
        "zin": two_parts(zin),
        "zout": two_parts(zout),
        "yin": two_parts(yin),
        "yout": two_parts(yout),
        "xin": four_parts(xin),
        "xout": four_parts(xout),
        "xmid": two_parts(xmid),
        "dy": two_parts(derivative_matrix(NY).T),
        "hy": two_parts(cas_matrix(NY)),
        "hx": four_parts(hx),
        "dz": dz,
        "along": along,
    }


def parts(values):
    high = values.astype(BF16)
    return high, (values - high.astype(F32)).astype(BF16)


def dot(a, b):
    return jnp.dot(a, b, preferred_element_type=F32)


def dot_t(a, b):
    return lax.dot_general(a, b, (((1,), (1,)), ((), ())), preferred_element_type=F32)


def table_first(table, values):
    high, low = parts(values)
    return dot(table[0], high) + dot(table[0], low) + dot(table[1], high)


def four_first(table, values):
    both = dot(table[...], jnp.concatenate(parts(values), axis=0))
    half = table.shape[0] // 2
    return both[:half] + both[half:]


def table_last(values, table):
    high, low = parts(values)
    return dot(high, table[0]) + dot(low, table[0]) + dot(high, table[1])


def one_hot(values, rows):
    places = lax.broadcasted_iota(jnp.int32, (rows, values.shape[1]), 0)
    return jnp.where(places == values, 1.0, 0.0)


def xc_terms(rho, g):
    kappa, mu = 0.804, 0.2195
    exch = 0.75 * (3.0 / math.pi) ** (1.0 / 3.0)
    scale = 1.0 / (4.0 * (3.0 * math.pi**2) ** (2.0 / 3.0))
    root = jnp.exp(jnp.log(rho) * (1.0 / 3.0))
    root = root - (root * root * root - rho) / (3.0 * root * root)
    four = rho * root
    s2 = scale * g / (four * four)
    q = 1.0 / (1.0 + s2 * (mu / kappa))
    enhance = 1.0 + kappa - kappa * q
    radius = (3.0 / (4.0 * math.pi)) ** (1.0 / 3.0) / root
    inverse = 1.0 / (7.8 + radius)
    v_local = -exch * root * ((4.0 / 3.0) * enhance - (8.0 / 3.0) * mu * s2 * q * q)
    v_local = v_local - 0.44 * inverse - (0.44 / 3.0) * radius * inverse * inverse
    return v_local, (-2.0 * exch * mu * scale) * q * q / four


def tiles(block, count):
    return jnp.concatenate([block[:, z * 128 : z * 128 + 128] for z in range(8)], axis=0)


def untile(rows, count):
    return jnp.concatenate([rows[z * count : z * count + count] for z in range(8)], axis=1)


def partner(place, ring, pair):
    return lax.rem(place // 2 + ring, 4) * 2 + lax.rem(place + pair, 2)


FIRST = ("coeffs", "mask", "zin")
LOADED = FIRST + ("cols", "dz", "yin", "xin", "core", "xmid", "dy", "hy", "hx", "xout", "yout")


def step_kernel(along, *refs):
    away, (back, *refs) = refs[: len(LOADED)], refs[len(LOADED) :]
    work(along, away, back, refs[: len(LOADED)], *refs[len(LOADED) :])


def work(
    along, away, back, near_by,
    aboves, belows, held, sticks, grid, psi, partial, summed, given,
    block, flux_x, flux_z, rho_hat, near_own, far_own, to_twin, from_twin,
    crossed, by_x, by_x2, by_z, by_z2, by_z3, kernel_z, near, far, pot, pot_twin, picked,
    kernel_sem, load_sem, send, recv,
):
    s, p = lax.axis_index("state"), lax.axis_index("plane")
    band, half = s // 2, lax.rem(s, 2)
    twin = 1 - half

    def on_plane(ring, pair):
        return {"state": s, "plane": partner(p, ring, pair)}

    def on_band(ring, pair):
        return {"state": partner(band, ring, pair) * 2 + half, "plane": p}

    on_twin = {"state": band * 2 + twin, "plane": p}

    barrier = pltpu.get_barrier_semaphore()
    for to in [on_twin] + [on_plane(*step) for step in STEPS] + [on_band(*step) for step in STEPS]:
        pl.semaphore_signal(barrier, inc=1, device_id=to, device_id_type=MESH)

    loads = {}
    for at, name in enumerate(LOADED):
        loads[name] = pltpu.make_async_copy(away[at], near_by[at], load_sem.at[at])
    for name in FIRST:
        loads[name].start()

    def loaded(*names):
        for name in names:
            loads[name].wait()
        return [near_by[LOADED.index(name)] for name in names]

    sent, received = [], [0]

    class Exchange:
        def __init__(self, copies, span, each=False):
            self.span, self.each, self.first = span, each, received[0]
            received[0] += len(copies) if each else 1
            self.copies = []
            for at, (src, dst, to) in enumerate(copies):
                copy = pltpu.make_async_remote_copy(
                    src_ref=src,
                    dst_ref=dst,
                    send_sem=send.at[len(sent)],
                    recv_sem=recv.at[self.first + at * each],
                    device_id=to,
                    device_id_type=MESH,
                )
                copy.start()
                self.copies.append(copy)
            sent.append(span)

        def wait(self, at=None):
            if at is None:
                pltpu.make_async_copy(self.span, self.span, recv.at[self.first]).wait()
            else:
                self.copies[at].wait_recv()

    def swap(src, dst, to):
        return Exchange([(src, dst, to)], dst)

    def rows_of(other):
        return pl.ds(pl.multiple_of(other * 8, 8), 8)

    def lanes_of(part):
        return pl.ds(pl.multiple_of(part * 1024, 1024), 1024)

    coeffs, mask, zin = loaded("coeffs", "mask", "zin")
    for name in LOADED[len(FIRST) :]:
        loads[name].start()
    fetch = pltpu.make_async_copy(along.at[band], kernel_z, kernel_sem)
    fetch.start()
    values = (coeffs[...] * mask[...].astype(F32)[None]).reshape(2 * NZ, CHUNK)
    held[...] = table_first(zin, values).reshape(PLANES, 32, CHUNK)
    pl.semaphore_wait(barrier, 15)
    arrivals = Exchange(
        [(held.at[partner(p, *step)], sticks.at[at], on_plane(*step)) for at, step in enumerate(STEPS)], sticks, True
    )

    cols, = loaded("cols")

    for chunk in range(PLANES):
        col = cols[:, chunk * CHUNK : chunk * CHUNK + CHUNK]
        aboves[chunk] = one_hot(col >> 8, 32).astype(BF16)
        belows[chunk] = one_hot(col & 255, 256).astype(BF16)

    def place(values, chunk, fresh):
        above, below = aboves[chunk][None], belows[chunk]
        high, low = parts(values)
        below = jnp.concatenate([below, below], axis=1)
        for first in (0, 16):
            left = jnp.concatenate(
                [(part[first : first + 16, None, :] * above).reshape(512, CHUNK) for part in (high, low)], axis=1
            )
            rows = slice(first * 32, first * 32 + 512)
            if fresh:
                grid[rows] = dot_t(left, below)
            else:
                grid[rows] += dot_t(left, below)

    place(held[p], p, True)
    for at, (ring, pair) in reversed(list(enumerate(STEPS))):
        arrivals.wait(at)
        place(sticks[at], partner(p, 4 - ring, pair), False)

    yin, xin, core, xmid = loaded("yin", "xin", "core", "xmid")
    def waves(part, quarter):
        lines = []
        for odd in range(2):
            rows = [
                grid[
                    pl.ds(pl.multiple_of(c * 512 + part * 256 + quarter * 128, 128), 128),
                    odd * 128 : odd * 128 + 128,
                ]
                for c in range(2)
            ]
            turned = table_last(jnp.concatenate(rows, axis=1), yin)
            lines.append(
                [
                    jnp.concatenate(
                        [turned[z * 32 : z * 32 + 32, c * 128 : c * 128 + 128] for z in range(4)], axis=1
                    )
                    for c in range(2)
                ]
            )
        lines = jnp.concatenate([lines[odd][c] for c in range(2) for odd in range(2)], axis=0)
        wave = four_first(xin, lines)
        psi[:, pl.ds(pl.multiple_of(part * 1024 + quarter * 512, 512), 512)] = wave
        return (wave[:64] * wave[:64] + wave[64:] * wave[64:]) * (1.0 / STATES)

    cuts = [slice(0, 512), slice(512, 1024)]
    swaps = []
    for quarter, cut in enumerate(cuts):
        to_twin[:, cut] = waves(twin, quarter)
        swaps.append(swap(to_twin.at[:, cut], from_twin.at[:, cut], on_twin))

    sums = []
    for quarter, cut in enumerate(cuts):
        own = waves(half, quarter)
        swaps[quarter].wait()
        summed[:, cut] = own + from_twin[:, cut]
        sums.append(
            Exchange(
                [
                    (summed.at[rows_of(partner(band, *step)), cut], given.at[at, :, cut], on_band(*step))
                    for at, step in enumerate(STEPS)
                ],
                given.at[:, :, cut],
            )
        )
    rho = jnp.concatenate([core[half * 8 + z, rows_of(band), :] for z in range(8)], axis=1)
    rho = rho + summed[rows_of(band), :]
    for part in sums:
        part.wait()
    for at in range(len(STEPS)):
        rho = rho + given[at]
    block[...] = rho

    def all_bands(src, dst):
        copies = [(src, dst.at[rows_of(band), :], on_band(*step)) for step in STEPS]
        return Exchange(copies, dst.at[pl.ds(0, 56), :])

    def all_planes(src, dst):
        copies = [(src, dst.at[at], on_plane(*step)) for at, step in enumerate(STEPS)]
        return [Exchange(copies[cut], dst.at[cut]) for cut in (slice(0, 4), slice(4, 7))]

    class Along:
        def __init__(self, own, arrivals, source, weight, slot):
            self.arrivals, self.source, self.weight, self.slot = arrivals, source, weight, slot
            self.left = [slice(0, 4), slice(4, 7)]
            self.sums = [[jnp.zeros((8, 128), F32)] * 8 for _ in range(2)]
            self.add(own, p)

        def add(self, planes, other):
            held = [planes[:, z * 128 : z * 128 + 128] for z in range(8)]
            for sums, part in zip(self.sums, (half, twin)):
                start = (p - other) * 16 + (part - half) * 8 + 128
                factors = {shift: self.weight(start + shift) for shift in range(-7, 8)}
                for to in range(8):
                    for z in range(8):
                        sums[to] = sums[to] + factors[to - z] * held[z]

        def take(self):
            cut = self.left.pop()
            self.arrivals.pop().wait()
            for at, (ring, pair) in reversed(list(enumerate(STEPS))[cut]):
                self.add(self.source[at], partner(p, 4 - ring, pair))

        def swap(self):
            while self.left:
                self.take()
            partial[self.slot, 0] = jnp.concatenate(self.sums[1], axis=1)
            self.copy = swap(partial.at[self.slot, 0], partial.at[self.slot, 1], on_twin)

        def result(self):
            self.copy.wait()
            return jnp.concatenate(self.sums[0], axis=1) + partial[self.slot, 1]

    def slope(at):
        return dz[at]

    def all_ring(src, dst):
        steps = [step for step in STEPS if step[1] == 0]
        copies = [(src, dst.at[at], on_band(*step)) for at, step in enumerate(steps)]
        return Exchange(copies, dst)

    def mix_x(own, source, slot, count):
        high, low = parts(jnp.concatenate([own] + [source[at] for at in range(3)], axis=0))
        both = dot(xmid[0, band], high) + dot(xmid[0, band], low) + dot(xmid[1, band], high)
        crossed[slot, 0, :count] = both[16 : 16 + count]
        copy = swap(crossed.at[slot, 0, :count], crossed.at[slot, 1, :count], on_band(0, 1))

        def result():
            copy.wait()
            return both[:count] + crossed[slot, 1, :count]

        return result

    dz, dy, hy, hx, xout, yout = loaded("dz", "dy", "hy", "hx", "xout", "yout")
    ring, planes = all_ring(block, by_x), all_planes(block, by_z)
    grad_z = Along(rho, planes, by_z, slope, 0)
    grad_y = untile(table_last(tiles(rho, 8), dy), 8)
    ring.wait()
    both = mix_x(rho, by_x, 0, 16)
    grad_z.take()
    both = both()
    grad_x = both[:8]
    rho_xy = untile(table_last(tiles(both[8:], 8), hy), 8)
    rho_hat[...] = rho_xy
    planes = all_planes(rho_hat, by_z3)
    grad_z.swap()
    fetch.wait()

    def even(at):
        at = lax.rem(at, 128)
        return kernel_z[jnp.minimum(at, 128 - at)]

    spread = Along(rho_xy, planes, by_z3, even, 1)
    grad_z = grad_z.result()

    v_local, twice = xc_terms(rho, grad_z * grad_z + grad_x * grad_x + grad_y * grad_y)
    along_x, across = twice * grad_x, twice * grad_z
    flux_x[...] = along_x
    ring = all_ring(flux_x, by_x2)
    flux_z[...] = across
    planes = all_planes(flux_z, by_z2)
    total = v_local - untile(table_last(tiles(twice * grad_y, 8), dy), 8)

    slant = Along(across, planes, by_z2, slope, 2)
    spread.swap()
    ring.wait()
    slope_x = mix_x(along_x, by_x2, 1, 8)
    spread = spread.result()
    far_own[...] = spread
    fars = all_bands(far_own, far)
    far[rows_of(band), :] = spread
    slant.swap()
    total = total - slope_x()
    total = total - slant.result()
    near_own[...] = total
    nears = all_bands(near_own, near)
    near[rows_of(band), :] = total

    fars.wait()
    turned = untile(table_last(tiles(four_first(hx, far[...]), 64), hy), 64)
    nears.wait()
    pot[...] = near[...] + turned
    copy = swap(pot, pot_twin, on_twin)

    def forces(potential, part):
        lanes = lanes_of(part)
        wave = psi[:, lanes]
        wave = jnp.concatenate([potential * wave[:64], potential * wave[64:]], axis=0)
        wave = four_first(xout, wave)
        for odd in range(2):
            rows = []
            for c in range(2):
                first = c * 64 + odd * 32
                rows.append(
                    jnp.concatenate([wave[first : first + 32, z * 128 : z * 128 + 128] for z in range(8)], axis=0)
                )
            turned = table_last(jnp.concatenate(rows, axis=1), yout)
            for c in range(2):
                at = pl.ds(pl.multiple_of(c * 512 + part * 256, 256), 256)
                grid[at, odd * 128 : odd * 128 + 128] = turned[:, c * 128 : c * 128 + 128]

    order = STEPS + ((0, 0),)

    def places_of(steps):
        owners = [partner(p, *step) for step in steps]
        above = jnp.concatenate([aboves[owner].astype(F32) for owner in owners], axis=1)
        below = jnp.concatenate([belows[owner] for owner in owners], axis=1)
        return owners, above[None], jnp.concatenate([below, below], axis=0)

    def pick(at, above, below):
        rows = grid[at, :]
        found = dot(jnp.concatenate(parts(rows), axis=1), below)
        return jnp.sum(found.reshape(-1, 32, found.shape[1]) * above, axis=1)

    def pick_half(owners, above, below, part):
        for c in range(2):
            found = pick(pl.ds(pl.multiple_of(c * 512 + part * 256, 256), 256), above, below)
            for at, owner in enumerate(owners):
                picked[owner, pl.ds(pl.multiple_of(c * 16 + part * 8, 8), 8), :] = found[
                    :, at * CHUNK : (at + 1) * CHUNK
                ]

    forces(pot[...], half)
    ahead = places_of(order[:1])
    pick_half(*ahead, half)
    copy.wait()
    forces(pot_twin[...], twin)
    pick_half(*ahead, twin)
    arrived = received[0]
    returns = []

    def give(step, owner):
        if step == (0, 0):
            copy = pltpu.make_async_copy(picked.at[p], back.at[p], kernel_sem)
        else:
            copy = pltpu.make_async_remote_copy(
                src_ref=picked.at[owner],
                dst_ref=back.at[p],
                send_sem=send.at[len(sent)],
                recv_sem=recv.at[arrived],
                device_id=on_plane(*step),
                device_id_type=MESH,
            )
        copy.start()
        returns.append(copy)

    give(order[0], ahead[0][0])
    for first in range(1, PLANES, 2):
        steps = order[first : first + 2]
        owners, above, below = places_of(steps)
        for c in range(2):
            found = pick(slice(c * 512, c * 512 + 512), above, below)
            for at, owner in enumerate(owners):
                picked[owner, c * 16 : c * 16 + 16, :] = found[:, at * CHUNK : (at + 1) * CHUNK]
        for step, owner in zip(steps, owners):
            give(step, owner)
    returns[-1].wait()
    seven = back.at[pl.ds(0, 7)]
    pltpu.make_async_copy(seven, seven, recv.at[arrived]).wait()
    for at, span in enumerate(sent + [seven]):
        pltpu.make_async_copy(span, span, send.at[at]).wait()


def last_kernel(back, mask, zout, out):
    force = table_first(zout, back[...].reshape(256, CHUNK)).reshape(2, NZ, CHUNK)
    out[...] = force * mask[...].astype(F32)[None]


SENDS, ARRIVALS = 22, 28


def call(kernel, outs, ins, in_specs, out_specs, scratch=(), collective=None, kib=60 * 1024):
    return pl.pallas_call(
        kernel,
        out_shape=[jax.ShapeDtypeStruct(shape, F32) for shape in outs],
        in_specs=in_specs,
        out_specs=out_specs,
        scratch_shapes=scratch,
        compiler_params=pltpu.CompilerParams(
            collective_id=collective,
            has_side_effects=collective is not None,
            vmem_limit_bytes=kib * 1024,
        ),
    )(*ins)


def on_device(coeffs, mask, stick_cols, core):
    t = {name: jnp.asarray(table) for name, table in tables().items()}
    t.update(coeffs=coeffs.reshape(2, NZ, CHUNK), mask=mask, cols=stick_cols.reshape(1, NSTICK), core=core)
    bundle, own, all_x, all_z = (PLANES, 32, CHUNK), (8, 1024), (64, 1024), (7, 8, 1024)
    shapes = [bundle, (7, 32, CHUNK), (1024, 256), (128, 2048), (3, 2, 8, 1024), all_x, all_z]
    shapes += [own] * 6 + [all_x] * 2
    shapes += [(2, 2, 16, 1024)] + [(3, 8, 1024)] * 2 + [all_z] * 3 + [(65, 8, 128)] + [all_x] * 4 + [bundle]
    anywhere, whole = pl.BlockSpec(memory_space=pl.ANY), pl.BlockSpec(memory_space=pltpu.VMEM)
    back, = call(
        step_kernel,
        [bundle],
        [t["along"]] + [t[name] for name in LOADED],
        [anywhere] * (len(LOADED) + 1),
        [anywhere],
        [
            (pltpu.SMEM if name == "dz" else pltpu.VMEM)(t[name].shape, t[name].dtype)
            for name in LOADED
        ]
        + [pltpu.VMEM((PLANES, rows, CHUNK), BF16) for rows in (32, 256)]
        + [pltpu.VMEM(shape, F32) for shape in shapes]
        + [pltpu.SemaphoreType.DMA, pltpu.SemaphoreType.DMA((len(LOADED),))]
        + [pltpu.SemaphoreType.DMA((SENDS,)), pltpu.SemaphoreType.DMA((ARRIVALS,))],
        collective=0,
    )
    forces, = call(
        last_kernel,
        [(2, NZ, CHUNK)],
        [back, mask, t["zout"]],
        [whole] * 3,
        [whole],
        kib=54600,
    )
    return forces.reshape(2, 1, NZ, CHUNK)


def solution(mesh):
    in_specs = (P(None, "state", None, "plane"), P(None, "plane"), P(), P("plane", None, None))
    out_specs = P(None, "state", None, "plane")
    return jax.shard_map(
        on_device, mesh=mesh, in_specs=in_specs, out_specs=out_specs, check_vma=False
    )
```
